32 devices in a mesh: groups: 2 (over y), emit: 4 (over z), recv: 4 (over x, core).
Axes of the slice: x: 2, y: 2, z: 4, core: 2. Of those that a mesh axis runs over, the one named last changes fastest.
Arguments:
- positions: float32 [3, 8192], P(None, ('groups', 'emit', 'recv')), parts along dimension 1, may hold values from 0 to 1
- angles: float32 [2, 8192], P(None, ('groups', 'emit', 'recv')), parts along dimension 1, may hold values from -3.140625 to 3.140625
- areas: float32 [8192], P(('groups', 'emit', 'recv')), parts along dimension 0, may hold values from 0.00024414062 to 0.00390625
- emissivity: float32 [8192], P(('groups', 'emit', 'recv')), parts along dimension 0, may hold values from 0.1 to 0.9
- emission: float32 [32, 8192], P(None, ('groups', 'emit', 'recv')), parts along dimension 1, may hold values from 0.5 to 2
- radiosity_in: float32 [32, 8192], P(None, ('groups', 'emit', 'recv')), parts along dimension 1, may hold values from 0.2 to 2
- adjoint_in: float32 [32, 8192], P(None, ('groups', 'emit', 'recv')), parts along dimension 1, may hold values from 0 to 1.5
- visibility: int32 [64, 32], P(('groups', 'emit')), parts along dimension 0, may hold values 0 or 1
- inlet_patches: int32 [4096], P('groups'), parts along dimension 0, may hold values from 0 to 4095
- inlet_weights: float32 [32, 4096], P(None, 'groups'), parts along dimension 1, may hold values from 0.5 to 2
Outputs:
- radiosity_out: float32 [32, 8192], P(None, ('groups', 'emit', 'recv')), parts along dimension 1
- adjoint_out: float32 [32, 8192], P(None, ('groups', 'emit', 'recv')), parts along dimension 1
- emissivity_grad: float32 [8192], P(('groups', 'emit', 'recv')), parts along dimension 0
The draws below stay inside these ranges and needn't reach their ends.
There are 2 independent parts, one for each index of `groups`. The reference program is written for one: setup_inputs(seed, part) draws one part's arguments, and reference() takes and returns one part's arrays. A program takes and returns all parts, laid end to end along the dimension named above; each array names one. Nothing has to cross between parts.
Inputs may be any that keep to these rules, and one draw needn't show every extreme that they name: `inlet_patches`: an inlet patch may be listed more than once.
All inputs are finite; a program needn't handle non-finite values. No bound on the sum of `visibility` on one device may be relied on, other than what follows from the above.
Results may differ from the reference program's by a relative error of at most 0.0003.
Values may be sent and summed in bfloat16 or wider, within the bound.
No kernel may reach another device: no remote copies, remote signals or barrier semaphores. Data moves between devices by JAX's collectives and lax.ppermute only.
A program may use at most 64 MiB of HBM per device.

```python
import math
import jax
import jax.numpy as jnp
from jax import lax

BLK = 128
CASES = 32
M_IN = 2048
NPATCH = 4096
NB = 32


def with_ends(entries, key, least, high):
    spot = [jax.random.randint(jax.random.fold_in(key, axis), (), 0, length) for axis, length in enumerate(entries.shape)]
    main_axis = entries.shape.index(max(entries.shape))
    next_to = spot[:main_axis] + [(spot[main_axis] + 1) % entries.shape[main_axis]] + spot[main_axis + 1:]
    return entries.at[tuple(spot)].set(least).at[tuple(next_to)].set(high)


def block_levels(rng, extent, shards, low, largest):
    factor_of, own = 1.0, jax.random.fold_in(rng, 6)
    for dim, blocks in shards:
        draws = jnp.exp(jax.random.uniform(jax.random.fold_in(own, dim), (blocks,), jnp.float32, low / len(shards), largest / len(shards)))
        factor_of = factor_of * jnp.repeat(draws, extent[dim] // blocks).reshape([-1 if axis == dim else 1 for axis in range(len(extent))])
    return factor_of


def setup_inputs(seed: int = 0, part: int = 0) -> dict:
    splits = jax.random.split(jax.random.key(seed), 11)
    part_keys = jax.random.split(jax.random.fold_in(splits[10], part), 11)
    positions = jnp.clip(1.0 * jax.random.uniform(part_keys[0], (3, NPATCH), jnp.float32) ** block_levels(part_keys[0], (3, NPATCH), ((1, 16),), -0.2, 0.2), 0.0, 1.0)
    angles = jnp.clip(jax.random.uniform(part_keys[1], (2, NPATCH), jnp.float32, -3.140625, 3.140625), -3.140625, 3.140625)
    areas = jnp.clip(jnp.exp(math.log(0.00390625) - 2.7725887 * jax.random.uniform(part_keys[2], (NPATCH,), jnp.float32) ** block_levels(part_keys[2], (NPATCH,), ((0, 16),), -0.2, 0.2)), 0.00024414062, 0.00390625)
    emissivity = jnp.clip(0.1 + 0.79999997 * jax.random.uniform(part_keys[3], (NPATCH,), jnp.float32) ** block_levels(part_keys[3], (NPATCH,), ((0, 16),), -0.2, 0.2), 0.1, 0.9)
    emission = jnp.clip(0.5 + 1.5 * jax.random.uniform(part_keys[4], (CASES, NPATCH), jnp.float32) ** block_levels(part_keys[4], (CASES, NPATCH), ((1, 16),), -0.2, 0.2), 0.5, 2.0)
    radiosity_in = jnp.clip(0.2 + 1.8 * jax.random.uniform(part_keys[5], (CASES, NPATCH), jnp.float32) ** block_levels(part_keys[5], (CASES, NPATCH), ((1, 16),), -0.2, 0.2), 0.2, 2.0)
    adjoint_in = jnp.clip(1.5 * jax.random.uniform(part_keys[6], (CASES, NPATCH), jnp.float32) ** block_levels(part_keys[6], (CASES, NPATCH), ((1, 16),), -0.2, 0.2), 0.0, 1.5)
    visibility = with_ends((jax.random.randint(part_keys[7], (NB, NB), 0, 4) < 3).astype(jnp.int32), jax.random.fold_in(part_keys[7], 1), 0, 1)
    inlet_patches = with_ends(jax.random.randint(part_keys[8], (M_IN,), 0, NPATCH), jax.random.fold_in(part_keys[8], 1), 0, NPATCH - 1).astype(jnp.int32)
    inlet_weights = jnp.clip(jax.random.uniform(part_keys[9], (CASES, M_IN), jnp.float32, 0.5, 2.0), 0.5, 2.0)
    return {"positions": positions, "angles": angles, "areas": areas, "emissivity": emissivity, "emission": emission, "radiosity_in": radiosity_in, "adjoint_in": adjoint_in, "visibility": visibility, "inlet_patches": inlet_patches, "inlet_weights": inlet_weights}


def patch_geometry(positions, angles, areas):
    polar = angles[0]
    azimuth = angles[1]
    normal = jnp.stack([jnp.sin(polar) * jnp.cos(azimuth), jnp.sin(polar) * jnp.sin(azimuth), jnp.cos(polar)])
    return jnp.concatenate([positions, normal, areas[None, :]], axis=0)


def view_tile(row_geom, col_geom, block_mask):
    delta_x = col_geom[0][None, :] - row_geom[0][:, None]
    delta_y = col_geom[1][None, :] - row_geom[1][:, None]
    delta_z = col_geom[2][None, :] - row_geom[2][:, None]
    dist_sq = delta_x * delta_x + delta_y * delta_y + delta_z * delta_z
    cos_emit = jnp.maximum(row_geom[3][:, None] * delta_x + row_geom[4][:, None] * delta_y + row_geom[5][:, None] * delta_z, 0.0)
    cos_recv = jnp.maximum(-(col_geom[3][None, :] * delta_x + col_geom[4][None, :] * delta_y + col_geom[5][None, :] * delta_z), 0.0)
    patch_area = row_geom[6][:, None]
    spread = dist_sq + patch_area
    kernel = cos_emit * cos_recv * patch_area / (math.pi * spread * spread)
    row_blocks, col_blocks = block_mask.shape
    rows_total = row_geom.shape[1]
    cols_total = col_geom.shape[1]
    expanded = jnp.broadcast_to(block_mask[:, None, :, None], (row_blocks, rows_total // row_blocks, col_blocks, cols_total // col_blocks)).reshape(rows_total, cols_total)
    return (expanded * kernel).astype(jnp.bfloat16)


def reference(positions, angles, areas, emissivity, emission, radiosity_in, adjoint_in, visibility, inlet_patches, inlet_weights):
    geometry = patch_geometry(positions, angles, areas)
    reflect = 1.0 - emissivity
    weighted = lax.optimization_barrier((reflect[None, :] * adjoint_in).astype(jnp.bfloat16)).astype(jnp.float32)
    values = lax.optimization_barrier(radiosity_in.astype(jnp.bfloat16)).astype(jnp.float32)
    full_mask = visibility.astype(jnp.float32)
    step_rows = 256
    block_count = NPATCH // step_rows

    def sweep_rows(forward, number):
        first = (number * step_rows).astype(jnp.int32)
        row_geom = lax.dynamic_slice_in_dim(geometry, first, step_rows, 1)
        mask_part = lax.dynamic_slice_in_dim(full_mask, first // BLK, step_rows // BLK, 0)
        tile = lax.optimization_barrier(view_tile(row_geom, geometry, mask_part)).astype(jnp.float32)
        value_part = lax.dynamic_slice_in_dim(values, first, step_rows, 1)
        forward = forward + jnp.dot(value_part, tile, precision=lax.Precision.HIGHEST, preferred_element_type=jnp.float32)
        adjoint_part = jnp.dot(weighted, tile.T, precision=lax.Precision.HIGHEST, preferred_element_type=jnp.float32)
        return forward, adjoint_part

    start_state = jnp.zeros((CASES, NPATCH), jnp.float32)
    incoming, pieces = lax.scan(sweep_rows, start_state, jnp.arange(block_count, dtype=jnp.int32))
    returned = jnp.transpose(pieces, (1, 0, 2)).reshape(CASES, NPATCH)
    source = jnp.zeros((CASES, NPATCH), jnp.float32).at[:, inlet_patches].add(inlet_weights)
    radiosity_out = emissivity[None, :] * emission + reflect[None, :] * incoming
    adjoint_out = source + returned
    emissivity_grad = jnp.sum(adjoint_out * (emission - incoming), axis=0)
    return (radiosity_out, adjoint_out, emissivity_grad)
```

```python
import functools
import math

import jax
import jax.numpy as jnp
import numpy as np
from jax import lax
from jax.experimental import pallas as pl
from jax.experimental.pallas import tpu as pltpu
from jax.sharding import PartitionSpec as P

BLK = 128
GEO = 32
FEAT = 128
ROWS = 32
NT = (((1,), (1,)), ((), ()))
TN = (((0,), (0,)), ((), ()))


def selection():
    pick = np.zeros((GEO, 2 * FEAT + 4 * BLK), np.float32)
    for part in range(3):
        base = part * GEO
        for split in range(3):
            for axis in range(3):
                pick[9 + 3 * part + axis, base + 3 * split + axis] = 1.0
                pick[3 * part + axis, FEAT + base + 9 + 3 * split + axis] = 1.0
        pick[18 + part, base + 21] = 1.0
        pick[21, FEAT + 18 + part] = 1.0
        for axis in range(3):
            first = 2 * FEAT + axis * BLK
            pick[3 * part + axis, first : first + BLK] = 1.0
        first = 2 * FEAT + 3 * BLK
        pick[22 + part, first : first + BLK] = 1.0
    return pick


def parts(x):
    high = x.astype(jnp.bfloat16).astype(jnp.float32)
    rest = x - high
    middle = rest.astype(jnp.bfloat16).astype(jnp.float32)
    return high, middle, rest - middle


def pack_kernel(positions, angles, areas, emissivity, radiosity, adjoint, row_ref, col_ref, geo):
    place = positions[...]
    turn = angles[...]
    sines = jnp.sin(turn)
    cosines = jnp.cos(turn)
    normal = jnp.concatenate(
        [sines[0:1] * cosines[1:2], sines[0:1] * sines[1:2], cosines[0:1]], axis=0
    )
    product = normal * place
    offset = -(product[0:1] + product[1:2] + product[2:3])
    geo[...] = jnp.zeros_like(geo)
    for number, (a, b, c, d) in enumerate(
        zip(parts(place), parts(normal), parts(offset), parts(areas[...]))
    ):
        geo[3 * number : 3 * number + 3, :] = a
        geo[9 + 3 * number : 12 + 3 * number, :] = b
        geo[18 + number : 19 + number, :] = c
        geo[22 + number : 23 + number, :] = d
    geo[21:22, :] = jnp.ones_like(offset)
    packed = geo[...].astype(jnp.bfloat16)
    cases = radiosity.shape[0]
    row_ref[0:cases, :] = radiosity[...].astype(jnp.bfloat16)
    row_ref[cases:, :] = packed
    col_ref[0:cases, :] = ((1.0 - emissivity[...]) * adjoint[...]).astype(jnp.bfloat16)
    col_ref[cases:, :] = packed


def source_kernel(ids, weights, out_ref, *, axes):
    own = out_ref.shape[1]
    first = (lax.axis_index(axes[0]) * lax.axis_size(axes[1]) + lax.axis_index(axes[1])) * own
    local = ids[...] - first
    step = 512
    total = jnp.zeros(out_ref.shape, jnp.float32)
    for start in range(0, ids.shape[1], step):
        here = local[:, start : start + step]
        hit = lax.broadcasted_iota(jnp.int32, (own, step), 0) == here
        chosen = jnp.where(hit, 1.0, 0.0).astype(jnp.bfloat16)
        for piece in parts(weights[:, start : start + step]):
            total = total + lax.dot_general(
                piece.astype(jnp.bfloat16), chosen, NT, preferred_element_type=jnp.float32
            )
    out_ref[...] = total


def tile_kernel(*refs, nr, nz):
    pick, seen = refs[0], refs[1]
    rows = refs[2 : 2 + nr]
    cols = refs[2 + nr : 2 + nr + nz]
    fwd = refs[2 + nr + nz : 2 + nr + 2 * nz]
    adj = refs[2 + nr + 2 * nz : 2 + 2 * nr + 2 * nz]
    left, wide, values, right, weights, places, ce, cr, tile, fwd_sum, adj_sum = refs[2 + 2 * nr + 2 * nz :]
    me_r = lax.axis_index("recv")
    me_z = lax.axis_index("emit")
    own = rows[0].shape[1]
    cases = rows[0].shape[0] - GEO
    for s in range(nr):
        feature = lax.dot_general(rows[s][cases:, :], pick[...], TN, preferred_element_type=jnp.float32)
        left[s] = feature[:, : 2 * FEAT].astype(jnp.bfloat16)
        wide[s, :, : 3 * BLK] = feature[:, 2 * FEAT : 2 * FEAT + 3 * BLK]
        wide[s, :, 3 * BLK :] = feature[:, 2 * FEAT + 3 * BLK :]
        values[s] = rows[s][0:cases, :]
        adj_sum[s] = jnp.zeros((cases, own), jnp.float32)
    for z in range(nz):
        geometry = cols[z][cases:, :]
        right[z] = jnp.concatenate([geometry, geometry, geometry, jnp.zeros_like(geometry)], axis=0)
        weights[z] = cols[z][0:cases, :]
        exact = geometry.astype(jnp.float32)
        places[z, 0:3, :] = exact[0:3] + exact[3:6] + exact[6:9]
        fwd_sum[z] = jnp.zeros((cases, own), jnp.float32)

    def pair(number, _):
        z = number // nr
        s = number % nr
        from_r = me_r ^ s
        to_z = me_z ^ z
        ce[...] = jnp.dot(left[s, :, :FEAT], right[z], preferred_element_type=jnp.float32)
        cr[...] = jnp.dot(left[s, :, FEAT:], right[z], preferred_element_type=jnp.float32)
        per = own // BLK
        for jb in range(per):
            lanes = slice(jb * BLK, (jb + 1) * BLK)
            xj = places[z, 0:1, lanes]
            yj = places[z, 1:2, lanes]
            zj = places[z, 2:3, lanes]
            for ib in range(per):
                sees = seen[from_r * per + ib, (to_z * nr + me_r) * per + jb].astype(jnp.float32)
                scale = sees * (1.0 / math.pi)
                for start in range(ib * BLK, (ib + 1) * BLK, ROWS):
                    here = slice(start, start + ROWS)
                    dx = wide[s, here, 0:BLK] - xj
                    dy = wide[s, here, BLK : 2 * BLK] - yj
                    dz = wide[s, here, 2 * BLK : 3 * BLK] - zj
                    area = wide[s, here, 3 * BLK :]
                    spread = dx * dx + dy * dy + dz * dz + area
                    product = jnp.maximum(ce[here, lanes], 0.0) * jnp.maximum(cr[here, lanes], 0.0)
                    view = product * (area * scale) / (spread * spread)
                    tile[here, lanes] = view.astype(jnp.bfloat16)
        fwd_sum[z] = fwd_sum[z] + jnp.dot(values[s], tile[...], preferred_element_type=jnp.float32)
        adj_sum[s] = adj_sum[s] + lax.dot_general(weights[z], tile[...], NT, preferred_element_type=jnp.float32)
        return 0

    lax.fori_loop(0, nr * nz, pair, 0)
    for s in range(nr):
        adj[s][...] = adj_sum[s]
    for z in range(nz):
        fwd[z][...] = fwd_sum[z]


def finish_kernel(*refs, nr, nz):
    emissivity, emission, source = refs[0:3]
    fwd = refs[3 : 3 + nz]
    adj = refs[3 + nz : 3 + nz + nr]
    radiosity_out, adjoint_out, gradient = refs[3 + nz + nr :]
    incoming = fwd[0][...]
    for piece in fwd[1:]:
        incoming = incoming + piece[...]
    returned = source[...]
    for piece in adj:
        returned = returned + piece[...]
    mine = emissivity[...]
    power = emission[...]
    radiosity_out[...] = mine * power + (1.0 - mine) * incoming
    adjoint_out[...] = returned
    gradient[...] = jnp.sum(returned * (power - incoming), axis=0, keepdims=True)


def swap(x, axis, other):
    if other == 0:
        return x
    return lax.ppermute(x, axis, [(i, i ^ other) for i in range(lax.axis_size(axis))])


def local(
    positions,
    angles,
    areas,
    emissivity,
    emission,
    radiosity_in,
    adjoint_in,
    visibility,
    inlet_patches,
    inlet_weights,
):
    nz = lax.axis_size("emit")
    nr = lax.axis_size("recv")
    own = areas.shape[0]
    cases = emission.shape[0]
    mine = emissivity.reshape(1, own)
    vmem = pl.BlockSpec(memory_space=pltpu.VMEM)
    smem = pl.BlockSpec(memory_space=pltpu.SMEM)
    packed = jax.ShapeDtypeStruct((cases + GEO, own), jnp.bfloat16)
    sums = jax.ShapeDtypeStruct((cases, own), jnp.float32)
    row_pack, col_pack = pl.pallas_call(
        pack_kernel,
        out_shape=(packed, packed),
        in_specs=[vmem] * 6,
        out_specs=(vmem, vmem),
        scratch_shapes=[pltpu.VMEM((GEO, own), jnp.float32)],
    )(positions, angles, areas.reshape(1, own), mine, radiosity_in, adjoint_in)
    rows = [swap(row_pack, "recv", k) for k in range(nr)]
    cols = [swap(col_pack, "emit", k) for k in range(nz)]
    source = pl.pallas_call(
        functools.partial(source_kernel, axes=("emit", "recv")),
        out_shape=sums,
        in_specs=[vmem] * 2,
        out_specs=vmem,
    )(inlet_patches.reshape(1, -1), inlet_weights)
    partial = pl.pallas_call(
        functools.partial(tile_kernel, nr=nr, nz=nz),
        out_shape=(sums,) * (nz + nr),
        in_specs=[vmem, smem] + [vmem] * (nr + nz),
        out_specs=(vmem,) * (nz + nr),
        scratch_shapes=[
            pltpu.VMEM((nr, own, 2 * FEAT), jnp.bfloat16),
            pltpu.VMEM((nr, own, 4 * BLK), jnp.float32),
            pltpu.VMEM((nr, cases, own), jnp.bfloat16),
            pltpu.VMEM((nz, FEAT, own), jnp.bfloat16),
            pltpu.VMEM((nz, cases, own), jnp.bfloat16),
            pltpu.VMEM((nz, 8, own), jnp.float32),
            pltpu.VMEM((own, own), jnp.float32),
            pltpu.VMEM((own, own), jnp.float32),
            pltpu.VMEM((own, own), jnp.bfloat16),
            pltpu.VMEM((nz, cases, own), jnp.float32),
            pltpu.VMEM((nr, cases, own), jnp.float32),
        ],
        compiler_params=pltpu.CompilerParams(vmem_limit_bytes=24 << 20),
    )(jnp.asarray(selection(), jnp.bfloat16), visibility, *rows, *cols)
    fwd = [swap(partial[k], "emit", k) for k in range(nz)]
    adj = [swap(partial[nz + k], "recv", k) for k in range(nr)]
    radiosity_out, adjoint_out, gradient = pl.pallas_call(
        functools.partial(finish_kernel, nr=nr, nz=nz),
        out_shape=(sums, sums, jax.ShapeDtypeStruct((1, own), jnp.float32)),
        in_specs=[vmem] * (3 + nz + nr),
        out_specs=(vmem, vmem, vmem),
    )(mine, emission, source, *fwd, *adj)
    return radiosity_out, adjoint_out, gradient.reshape(own)


def solution(mesh):
    patch = ("groups", "emit", "recv")
    placed = (
        P(None, patch),
        P(None, patch),
        P(patch),
        P(patch),
        P(None, patch),
        P(None, patch),
        P(None, patch),
        P(("groups", "emit"), None),
        P("groups"),
        P(None, "groups"),
    )
    return jax.shard_map(
        local,
        mesh=mesh,
        in_specs=placed,
        out_specs=(P(None, patch), P(None, patch), P(patch)),
        check_vma=False,
    )
```

```python
import functools
import math

import jax
import jax.numpy as jnp
import numpy as np
from jax import lax
from jax.experimental import pallas as pl
from jax.experimental.pallas import tpu as pltpu
from jax.sharding import PartitionSpec as P

BLK = 128
GEO = 24
SLAB = 32
FEAT = 128
ROWS = 32
NT = (((1,), (1,)), ((), ()))
TN = (((0,), (0,)), ((), ()))


def selection():
    pick = np.zeros((SLAB, 2 * FEAT + 4 * BLK), np.float32)
    for part in range(3):
        base = part * SLAB
        for split in range(3):
            for axis in range(3):
                pick[9 + 3 * part + axis, base + 3 * split + axis] = 1.0
                pick[3 * part + axis, FEAT + base + 9 + 3 * split + axis] = 1.0
        pick[18 + part, 3 * SLAB + part] = 1.0
        pick[24, FEAT + 18 + part] = 1.0
        for axis in range(3):
            first = 2 * FEAT + axis * BLK
            pick[3 * part + axis, first : first + BLK] = 1.0
        first = 2 * FEAT + 3 * BLK
        pick[21 + part, first : first + BLK] = 1.0
    return pick


def parts(x):
    high = x.astype(jnp.bfloat16).astype(jnp.float32)
    rest = x - high
    middle = rest.astype(jnp.bfloat16).astype(jnp.float32)
    return high, middle, rest - middle


def pack_kernel(*refs, nr, nz, held):
    given = refs[1 : 1 + held]
    target_ref = refs[1 + held]
    sources = refs[2 + held : 2 + held + nz]
    kept = refs[2 + held + nz : 2 + held + nz + 4]
    mask_ref = refs[2 + held + nz + 4]
    place_ref, turn_ref, area_ref, radiosity, adjoint, geo, seen, sems, seen_sem = refs[2 + held + nz + 5 :]
    emissivity_ref = kept[0]
    landing = (place_ref, turn_ref, area_ref, emissivity_ref, radiosity, adjoint) + tuple(kept[1:])
    copies = [pltpu.make_async_copy(a, b, sems.at[i]) for i, (a, b) in enumerate(zip(given, landing))]
    sight = pltpu.make_async_copy(refs[0], seen, seen_sem)
    sight.start()
    for copy in copies:
        copy.start()
    me_r = lax.axis_index("recv")
    me_z = lax.axis_index("emit")
    own = area_ref.shape[1]
    cases = radiosity.shape[0]
    per = own // BLK
    for copy in copies[:3]:
        copy.wait()
    place = place_ref[...]
    turn = turn_ref[...]
    sines = jnp.sin(turn)
    cosines = jnp.cos(turn)
    normal = jnp.concatenate(
        [sines[0:1] * cosines[1:2], sines[0:1] * sines[1:2], cosines[0:1]], axis=0
    )
    product = normal * place
    offset = -(product[0:1] + product[1:2] + product[2:3])
    for number, (a, b, c, d) in enumerate(
        zip(parts(place), parts(normal), parts(offset), parts(area_ref[...]))
    ):
        geo[0, 3 * number : 3 * number + 3, :] = a
        geo[0, 9 + 3 * number : 12 + 3 * number, :] = b
        geo[0, 18 + number : 19 + number, :] = c
        geo[0, 21 + number : 22 + number, :] = d
    sight.wait()
    for k in range(nz):
        for s in range(nr):
            for ib in range(per):
                row = GEO + s * per + ib
                col = ((me_z ^ k) * nr + (me_r ^ s)) * per + ib
                spot = (k * nr + s) * per + ib
                for jb in range(per):
                    lanes = slice(jb * BLK, (jb + 1) * BLK)
                    sees = seen[me_r * per + jb, col].astype(jnp.float32)
                    geo[k, row : row + 1, lanes] = jnp.full((1, BLK), sees, jnp.float32)
                    other = seen[(me_r ^ s) * per + ib, ((me_z ^ k) * nr + me_r) * per + jb]
                    sees = other.astype(jnp.float32) * (1.0 / math.pi)
                    mask_ref[spot : spot + 1, lanes] = jnp.full((1, BLK), sees, jnp.float32)
    shared = geo[0, 0:GEO, :]
    one = jnp.ones((SLAB - GEO, own), jnp.float32)
    target_ref[...] = jnp.concatenate([shared, one], axis=0).astype(jnp.bfloat16)
    for copy in copies[3:6]:
        copy.wait()
    value = radiosity[...].astype(jnp.bfloat16)
    weighted = ((1.0 - emissivity_ref[...]) * adjoint[...]).astype(jnp.bfloat16)
    for k in range(nz):
        sources[k][0:cases, :] = value
        sources[k][cases : 2 * cases, :] = weighted
        sources[k][2 * cases :, :] = jnp.concatenate([shared, geo[k, GEO:, :]], axis=0).astype(jnp.bfloat16)
    for copy in copies[6:]:
        copy.wait()


def source_kernel(ids, weights, out_ref):
    own = out_ref.shape[1]
    first = (lax.axis_index("emit") * lax.axis_size("recv") + lax.axis_index("recv")) * own
    half = out_ref.shape[0] // 2
    hit = lax.broadcasted_iota(jnp.int32, (own, ids.shape[1]), 0) == ids[...] - first
    chosen = jnp.where(hit, 1.0, 0.0).astype(jnp.bfloat16)
    pieces = jnp.concatenate(parts(weights[...]), axis=0).astype(jnp.bfloat16)
    split = lax.dot_general(pieces, chosen, NT, preferred_element_type=jnp.float32)
    out_ref[0:half, :] = jnp.zeros((half, own), jnp.float32)
    out_ref[half:, :] = split[0:half] + split[half : 2 * half] + split[2 * half :]


def one_row(ref, row, lanes):
    if isinstance(row, int):
        return ref[row : row + 1, lanes]
    around = ref[pl.ds(pl.multiple_of(row // 8 * 8, 8), 8), lanes]
    pick = lax.broadcasted_iota(jnp.int32, around.shape, 0) == row % 8
    return jnp.sum(jnp.where(pick, around, 0.0), axis=0, keepdims=True)


def prepare_kernel(*refs, count):
    pick = refs[0]
    targets = refs[1 : 1 + count]
    left, wide = refs[1 + count :]
    own = targets[0].shape[1]
    pair = left.shape[1] // own
    for g in range(count // pair):
        both = jnp.concatenate([targets[g * pair + t][...] for t in range(pair)], axis=1)
        feature = lax.dot_general(both, pick[...], TN, preferred_element_type=jnp.float32)
        left[g] = feature[:, : 2 * FEAT].astype(jnp.bfloat16)
        wide[g] = feature[:, 2 * FEAT :]


def sum_kernel(*refs, first, count, blocks, numbers):
    ns = len(numbers)
    mask, left, wide = refs[0:3]
    sources = refs[3 : 3 + ns]
    begin = refs[3 + ns : 3 + ns + count]
    out = refs[3 + ns + count : 3 + ns + 2 * count]
    facing, back, fwd_tile, adj_tile, total, stack, geo, scale_q = refs[3 + ns + 2 * count :]
    own = out[0].shape[1]
    cases = out[0].shape[0] // 2
    per = own // BLK
    span = left.shape[1]
    pair = span // own
    groups = count // pair
    for t in range(count):
        total[t] = begin[t][...]

    def match(k, g, slot, source):
        slab = source[2 * cases : 2 * cases + SLAB, :]
        right = jnp.concatenate([slab, slab, slab, jnp.ones_like(slab)], axis=0)
        facing[slot] = jnp.dot(left[g, :, :FEAT], right, preferred_element_type=jnp.float32)
        back[slot] = jnp.dot(left[g, :, FEAT:], right, preferred_element_type=jnp.float32)

    def measure(k, slot, source):
        exact = source[2 * cases :, :].astype(jnp.float32)
        geo[slot, 0:3, :] = exact[0:3] + exact[3:6] + exact[6:9]
        area_q = exact[21:22] + exact[22:23] + exact[23:24]
        geo[slot, 3:4, :] = area_q
        scale_q[slot] = exact[GEO:] * (area_q * (1.0 / math.pi))

    def build(k, g, slot, side):
        for jb in range(per):
            lanes = slice(jb * BLK, (jb + 1) * BLK)
            xq = geo[side, 0:1, lanes]
            yq = geo[side, 1:2, lanes]
            zq = geo[side, 2:3, lanes]
            aq = geo[side, 3:4, lanes]
            for block in range(pair * per):
                row = (first + g * pair) * per + block
                scale = one_row(scale_q.at[side], row, lanes)
                sees = one_row(mask, k * blocks + row, lanes)
                for start in range(block * BLK, (block + 1) * BLK, ROWS):
                    here = slice(start, start + ROWS)
                    dx = wide[g, here, 0:BLK] - xq
                    dy = wide[g, here, BLK : 2 * BLK] - yq
                    dz = wide[g, here, 2 * BLK : 3 * BLK] - zq
                    area = wide[g, here, 3 * BLK :]
                    square = dx * dx + dy * dy + dz * dz
                    product = jnp.maximum(facing[slot, here, lanes], 0.0) * jnp.maximum(back[slot, here, lanes], 0.0)
                    near = square + aq
                    far = square + area
                    fwd_tile[slot, here, lanes] = (product * scale / (near * near)).astype(jnp.bfloat16)
                    adj_tile[slot, here, lanes] = (product * sees * area / (far * far)).astype(jnp.bfloat16)

    def collect(g, slot, source):
        incoming = lax.dot_general(source[0:cases, :], fwd_tile[slot], NT, preferred_element_type=jnp.float32)
        returned = lax.dot_general(
            source[cases : 2 * cases, :], adj_tile[slot], NT, preferred_element_type=jnp.float32
        )
        for t in range(pair):
            s = g * pair + t
            total[s, 0:cases, :] += incoming[:, t * own : (t + 1) * own]
            total[s, cases:, :] += returned[:, t * own : (t + 1) * own]

    if ns * groups <= 8:
        steps = [(i, g) for i in range(ns) for g in range(groups)]
        for number, (i, g) in enumerate(steps):
            if number == 0:
                measure(numbers[i], i % 2, sources[i])
                match(numbers[i], g, 0, sources[i])
            if number + 1 < len(steps):
                j, h = steps[number + 1]
                if j != i:
                    measure(numbers[j], j % 2, sources[j])
                match(numbers[j], h, (number + 1) % 2, sources[j])
            build(numbers[i], g, number % 2, i % 2)
            collect(g, number % 2, sources[i])
    else:
        for i in range(ns):
            stack[i] = sources[i][...]

        def step(number, _):
            i, g = number // groups, number % groups
            source = stack.at[i]
            measure(numbers[0] + i, 0, source)
            match(numbers[0] + i, g, 0, source)
            build(numbers[0] + i, g, 0, 0)
            collect(g, 0, source)
            return 0

        lax.fori_loop(0, ns * groups, step, 0)
    for t in range(count):
        out[t][...] = total[t]


def finish_kernel(*refs, nr):
    emissivity, emission = refs[0:2]
    pieces = refs[2 : 2 + nr]
    radiosity_out, adjoint_out, gradient = refs[2 + nr :]
    cases = emission.shape[0]
    total = pieces[0][...]
    for piece in pieces[1:]:
        total = total + piece[...]
    incoming = total[0:cases]
    returned = total[cases:]
    mine = emissivity[...]
    power = emission[...]
    radiosity_out[...] = mine * power + (1.0 - mine) * incoming
    adjoint_out[...] = returned
    gradient[...] = jnp.sum(returned * (power - incoming), axis=0, keepdims=True)


def busy(micros):
    return pl.CostEstimate(flops=int(micros * 1.1e9), bytes_accessed=0, transcendentals=0)


def swap(x, axis, other):
    if other == 0:
        return x
    return lax.ppermute(x, axis, [(i, i ^ other) for i in range(lax.axis_size(axis))])


def local(
    positions,
    angles,
    areas,
    emissivity,
    emission,
    radiosity_in,
    adjoint_in,
    visibility,
    inlet_patches,
    inlet_weights,
):
    nz = lax.axis_size("emit")
    nr = lax.axis_size("recv")
    own = areas.shape[0]
    cases = emission.shape[0]
    per = own // BLK
    ids = inlet_patches.reshape(1, -1)
    vmem = pl.BlockSpec(memory_space=pltpu.VMEM)
    hbm = pl.BlockSpec(memory_space=pltpu.HBM)
    small = pltpu.CompilerParams(vmem_limit_bytes=4 << 20)
    f32 = jnp.float32
    blocks = nr * per
    rows = 2 * cases + GEO + blocks
    given = (
        positions,
        angles,
        areas.reshape(1, own),
        emissivity.reshape(1, own),
        radiosity_in,
        adjoint_in,
        emission,
        ids,
        inlet_weights,
    )
    given = tuple(pltpu.with_memory_space_constraint(x, pltpu.HBM) for x in given)
    seen = pltpu.with_memory_space_constraint(visibility, pltpu.HBM)
    packed = pl.pallas_call(
        functools.partial(pack_kernel, nr=nr, nz=nz, held=len(given)),
        out_shape=(jax.ShapeDtypeStruct((SLAB, own), jnp.bfloat16),)
        + (jax.ShapeDtypeStruct((rows, own), jnp.bfloat16),) * nz
        + tuple(jax.ShapeDtypeStruct(given[i].shape, given[i].dtype) for i in (3, 6, 7, 8))
        + (jax.ShapeDtypeStruct((nz * blocks, own), f32),),
        in_specs=[hbm] * (1 + len(given)),
        out_specs=(vmem,) * (1 + nz + 5),
        scratch_shapes=[
            pltpu.VMEM((3, own), f32),
            pltpu.VMEM((2, own), f32),
            pltpu.VMEM((1, own), f32),
            pltpu.VMEM((cases, own), f32),
            pltpu.VMEM((cases, own), f32),
            pltpu.VMEM((nz, GEO + blocks, own), f32),
            pltpu.SMEM(visibility.shape, jnp.int32),
            pltpu.SemaphoreType.DMA((len(given),)),
            pltpu.SemaphoreType.DMA,
        ],
        compiler_params=small,
    )(seen, *given)
    mine, power, ids, weights, mask = packed[1 + nz :]
    targets = []
    for s in range(nr):
        targets.append(swap(targets[s - 1], "recv", 1) if s % 2 else swap(packed[0], "recv", s))
    sources = [swap(packed[1 + k], "emit", k) for k in range(nz)]
    source = pl.pallas_call(
        source_kernel,
        out_shape=jax.ShapeDtypeStruct((2 * cases, own), f32),
        in_specs=[vmem] * 2,
        out_specs=vmem,
        compiler_params=small,
        cost_estimate=busy(0.5),
    )(ids, weights)
    pick = jnp.asarray(selection(), jnp.bfloat16)
    sums = jax.ShapeDtypeStruct((2 * cases, own), f32)
    zero = jnp.zeros((2 * cases, own), f32)

    def prepare(chosen):
        count = len(chosen)
        pair = min(count, 2)
        return pl.pallas_call(
            functools.partial(prepare_kernel, count=count),
            out_shape=(
                jax.ShapeDtypeStruct((count // pair, pair * own, 2 * FEAT), jnp.bfloat16),
                jax.ShapeDtypeStruct((count // pair, pair * own, 4 * BLK), f32),
            ),
            in_specs=[vmem] * (1 + count),
            out_specs=(vmem, vmem),
            compiler_params=small,
            cost_estimate=busy(0.2 * count),
        )(pick, *chosen)

    def add(first, shape, numbers, begin):
        count = len(begin)
        pair = min(count, 2)
        many = len(numbers) * (count // pair) > 8
        return list(
            pl.pallas_call(
                functools.partial(sum_kernel, first=first, count=count, blocks=blocks, numbers=numbers),
                out_shape=(sums,) * count,
                in_specs=[vmem] * (3 + len(numbers) + count),
                out_specs=(vmem,) * count,
                scratch_shapes=[
                    pltpu.VMEM((2, pair * own, own), f32),
                    pltpu.VMEM((2, pair * own, own), f32),
                    pltpu.VMEM((2, pair * own, own), jnp.bfloat16),
                    pltpu.VMEM((2, pair * own, own), jnp.bfloat16),
                    pltpu.VMEM((count, 2 * cases, own), f32),
                    pltpu.VMEM((len(numbers) if many else 1, rows, own), jnp.bfloat16),
                    pltpu.VMEM((2, 8, own), f32),
                    pltpu.VMEM((2, blocks, own), f32),
                ],
                compiler_params=pltpu.CompilerParams(vmem_limit_bytes=12 << 20),
                cost_estimate=busy(0.3 * count * len(numbers)),
            )(mask, *shape, *[sources[k] for k in numbers], *begin)
        )

    own_shape = prepare(targets[:1])
    core_shape = prepare(targets[1:2])
    far_shape = prepare(targets[2:])
    rest = tuple(range(1, nz))
    own_sums = add(0, own_shape, (0,), [source])
    core_sums = add(1, core_shape, (0,), [zero])
    far_sums = add(2, far_shape, (0,), [zero] * (nr - 2))
    core_sums = add(1, core_shape, rest, core_sums)
    far_sums, core_sums = lax.optimization_barrier((far_sums, core_sums))
    far_sums = add(2, far_shape, rest, far_sums)
    far_sums, own_sums = lax.optimization_barrier((far_sums, own_sums))
    own_sums = add(0, own_shape, rest, own_sums)
    pieces = [swap(x, "recv", s) for s, x in enumerate(own_sums + core_sums + far_sums)]
    whole = jax.ShapeDtypeStruct((cases, own), f32)
    radiosity_out, adjoint_out, gradient = pl.pallas_call(
        functools.partial(finish_kernel, nr=nr),
        out_shape=(whole, whole, jax.ShapeDtypeStruct((1, own), f32)),
        in_specs=[vmem] * (2 + nr),
        out_specs=(vmem, vmem, vmem),
        compiler_params=small,
    )(mine, power, *pieces)
    return radiosity_out, adjoint_out, gradient.reshape(own)


def solution(mesh):
    patch = ("groups", "emit", "recv")
    placed = (
        P(None, patch),
        P(None, patch),
        P(patch),
        P(patch),
        P(None, patch),
        P(None, patch),
        P(None, patch),
        P(("groups", "emit"), None),
        P("groups"),
        P(None, "groups"),
    )
    return jax.shard_map(
        local,
        mesh=mesh,
        in_specs=placed,
        out_specs=(P(None, patch), P(None, patch), P(patch)),
        check_vma=False,
    )
```

```python
import functools
import math

import jax
import jax.numpy as jnp
import numpy as np
from jax import lax
from jax.experimental import pallas as pl
from jax.experimental.pallas import tpu as pltpu
from jax.sharding import PartitionSpec as P

BLK = 128
GEO = 24
SLAB = 32
FEAT = 128
ROWS = 32
NT = (((1,), (1,)), ((), ()))
TN = (((0,), (0,)), ((), ()))


def selection():
    pick = np.zeros((SLAB, 2 * FEAT + 4 * BLK), np.float32)
    for part in range(3):
        base = part * SLAB
        for split in range(3):
            for axis in range(3):
                pick[9 + 3 * part + axis, base + 3 * split + axis] = 1.0
                pick[3 * part + axis, FEAT + base + 9 + 3 * split + axis] = 1.0
        pick[18 + part, 3 * SLAB + part] = 1.0
        pick[24, FEAT + 18 + part] = 1.0
        for axis in range(3):
            first = 2 * FEAT + axis * BLK
            pick[3 * part + axis, first : first + BLK] = 1.0
        first = 2 * FEAT + 3 * BLK
        pick[21 + part, first : first + BLK] = 1.0
    return pick


def parts(x):
    high = x.astype(jnp.bfloat16).astype(jnp.float32)
    rest = x - high
    middle = rest.astype(jnp.bfloat16).astype(jnp.float32)
    return high, middle, rest - middle


def pack_kernel(*refs, nr, nz, held):
    given = refs[1 : 1 + held]
    target_ref = refs[1 + held]
    sources = refs[2 + held : 2 + held + nz]
    kept = refs[2 + held + nz : 2 + held + nz + 4]
    mask_ref = refs[2 + held + nz + 4]
    place_ref, turn_ref, area_ref, radiosity, adjoint, geo, seen, sems, seen_sem = refs[2 + held + nz + 5 :]
    emissivity_ref = kept[0]
    landing = (place_ref, turn_ref, area_ref, emissivity_ref, radiosity, adjoint) + tuple(kept[1:])
    copies = [pltpu.make_async_copy(a, b, sems.at[i]) for i, (a, b) in enumerate(zip(given, landing))]
    sight = pltpu.make_async_copy(refs[0], seen, seen_sem)
    sight.start()
    for copy in copies:
        copy.start()
    me_r = lax.axis_index("recv")
    me_z = lax.axis_index("emit")
    own = area_ref.shape[1]
    cases = radiosity.shape[0]
    per = own // BLK
    for copy in copies[:3]:
        copy.wait()
    place = place_ref[...]
    turn = turn_ref[...]
    sines = jnp.sin(turn)
    cosines = jnp.cos(turn)
    normal = jnp.concatenate(
        [sines[0:1] * cosines[1:2], sines[0:1] * sines[1:2], cosines[0:1]], axis=0
    )
    product = normal * place
    offset = -(product[0:1] + product[1:2] + product[2:3])
    for number, (a, b, c, d) in enumerate(
        zip(parts(place), parts(normal), parts(offset), parts(area_ref[...]))
    ):
        geo[0, 3 * number : 3 * number + 3, :] = a
        geo[0, 9 + 3 * number : 12 + 3 * number, :] = b
        geo[0, 18 + number : 19 + number, :] = c
        geo[0, 21 + number : 22 + number, :] = d
    sight.wait()
    for k in range(nz):
        for s in range(nr):
            for ib in range(per):
                row = GEO + s * per + ib
                col = ((me_z ^ k) * nr + (me_r ^ s)) * per + ib
                spot = (k * nr + s) * per + ib
                for jb in range(per):
                    lanes = slice(jb * BLK, (jb + 1) * BLK)
                    sees = seen[me_r * per + jb, col].astype(jnp.float32)
                    geo[k, row : row + 1, lanes] = jnp.full((1, BLK), sees, jnp.float32)
                    other = seen[(me_r ^ s) * per + ib, ((me_z ^ k) * nr + me_r) * per + jb]
                    sees = other.astype(jnp.float32) * (1.0 / math.pi)
                    mask_ref[spot : spot + 1, lanes] = jnp.full((1, BLK), sees, jnp.float32)
    shared = geo[0, 0:GEO, :]
    one = jnp.ones((SLAB - GEO, own), jnp.float32)
    target_ref[...] = jnp.concatenate([shared, one], axis=0).astype(jnp.bfloat16)
    for copy in copies[3:6]:
        copy.wait()
    value = radiosity[...].astype(jnp.bfloat16)
    weighted = ((1.0 - emissivity_ref[...]) * adjoint[...]).astype(jnp.bfloat16)
    for k in range(nz):
        sources[k][0:cases, :] = value
        sources[k][cases : 2 * cases, :] = weighted
        sources[k][2 * cases :, :] = jnp.concatenate([shared, geo[k, GEO:, :]], axis=0).astype(jnp.bfloat16)
    for copy in copies[6:]:
        copy.wait()


def source_kernel(ids, weights, out_ref):
    own = out_ref.shape[1]
    first = (lax.axis_index("emit") * lax.axis_size("recv") + lax.axis_index("recv")) * own
    half = out_ref.shape[0] // 2
    hit = lax.broadcasted_iota(jnp.int32, (own, ids.shape[1]), 0) == ids[...] - first
    chosen = jnp.where(hit, 1.0, 0.0).astype(jnp.bfloat16)
    pieces = jnp.concatenate(parts(weights[...]), axis=0).astype(jnp.bfloat16)
    split = lax.dot_general(pieces, chosen, NT, preferred_element_type=jnp.float32)
    out_ref[0:half, :] = jnp.zeros((half, own), jnp.float32)
    out_ref[half:, :] = split[0:half] + split[half : 2 * half] + split[2 * half :]


def one_row(ref, row, lanes):
    if isinstance(row, int):
        return ref[row : row + 1, lanes]
    around = ref[pl.ds(pl.multiple_of(row // 8 * 8, 8), 8), lanes]
    pick = lax.broadcasted_iota(jnp.int32, around.shape, 0) == row % 8
    return jnp.sum(jnp.where(pick, around, 0.0), axis=0, keepdims=True)


def prepare_kernel(*refs, count):
    pick = refs[0]
    targets = refs[1 : 1 + count]
    left = refs[1 + count : 1 + 2 * count]
    wide = refs[1 + 2 * count :]
    own = targets[0].shape[1]
    both = jnp.concatenate([target[...] for target in targets], axis=1)
    feature = lax.dot_general(both, pick[...], TN, preferred_element_type=jnp.float32)
    for t in range(count):
        lines = slice(t * own, (t + 1) * own)
        left[t][...] = feature[lines, : 2 * FEAT].astype(jnp.bfloat16)
        wide[t][...] = feature[lines, 2 * FEAT :]


def sum_kernel(*refs, slots, blocks, numbers):
    ns, count = len(numbers), len(slots)
    refs = list(refs)

    def take(amount):
        taken = refs[:amount]
        del refs[:amount]
        return taken

    mask = take(1)[0]
    left, wide = take(count), take(count)
    sources = take(ns)
    begin, out = take(count), take(count)
    facing, back, fwd_tile, adj_tile = take(2), take(2), take(2), take(2)
    total, stack, geo, scale_q = refs
    own = out[0].shape[1]
    cases = out[0].shape[0] // 2
    per = own // BLK
    for t in range(count):
        total[t] = begin[t][...]

    def match(slot, source):
        slab = source[2 * cases : 2 * cases + SLAB, :]
        right = jnp.concatenate([slab, slab, slab, jnp.ones_like(slab)], axis=0)

        def piece(t, which):
            cols = slice(FEAT, 2 * FEAT) if which else slice(0, FEAT)
            (back if which else facing)[slot][t * own : (t + 1) * own, :] = jnp.dot(
                left[t][:, cols], right, preferred_element_type=jnp.float32
            )

        return [functools.partial(piece, t, which) for t in range(count) for which in (0, 1)]

    def measure(slot, source):
        exact = source[2 * cases :, :].astype(jnp.float32)
        geo[slot, 0:3, :] = exact[0:3] + exact[3:6] + exact[6:9]
        area_q = exact[21:22] + exact[22:23] + exact[23:24]
        geo[slot, 3:4, :] = area_q
        scale_q[slot] = exact[GEO:] * (area_q * (1.0 / math.pi))

    def build(k, slot, woven=()):
        spots, spot = count * own // ROWS, 0
        amount, done = len(woven), 0
        marks = []
        for jb in range(per):
            lanes = slice(jb * BLK, (jb + 1) * BLK)
            marks.append((lanes, [geo[slot, c : c + 1, lanes] for c in range(4)]))
        for t in range(count):
            for ib in range(per):
                row = slots[t] * per + ib
                pairs = [
                    (lanes, place, one_row(scale_q.at[slot], row, lanes), one_row(mask, k * blocks + row, lanes))
                    for lanes, place in marks
                ]
                for start in range(ib * BLK, (ib + 1) * BLK, ROWS):
                    here = slice(start, start + ROWS)
                    there = slice(t * own + start, t * own + start + ROWS)
                    x, y, z, area = (wide[t][here, c * BLK : (c + 1) * BLK] for c in range(4))
                    for lanes, (xq, yq, zq, aq), scale, sees in pairs:
                        dx = x - xq
                        dy = y - yq
                        dz = z - zq
                        square = dx * dx + dy * dy + dz * dz
                        faced = jnp.maximum(facing[slot][there, lanes], 0.0)
                        product = faced * jnp.maximum(back[slot][there, lanes], 0.0)
                        near = square + aq
                        far = square + area
                        fwd_tile[slot][there, lanes] = (product * scale / (near * near)).astype(jnp.bfloat16)
                        adj_tile[slot][there, lanes] = (product * sees * area / (far * far)).astype(jnp.bfloat16)
                    spot += 1
                    due = spot * amount // spots
                    while done < due:
                        woven[done]()
                        done += 1

    def collect(slot, source):
        def piece(t, which):
            lines = slice(cases, 2 * cases) if which else slice(0, cases)
            tile = (adj_tile if which else fwd_tile)[slot][t * own : (t + 1) * own, :]
            total[t, lines, :] += lax.dot_general(source[lines, :], tile, NT, preferred_element_type=jnp.float32)

        return [functools.partial(piece, t, which) for t in range(count) for which in (0, 1)]

    if ns <= 4:
        late = []
        for number, k in enumerate(numbers):
            if number == 0:
                measure(0, sources[0])
                for piece in match(0, sources[0]):
                    piece()
            if number + 1 < ns:
                measure((number + 1) % 2, sources[number + 1])
                late = late + match((number + 1) % 2, sources[number + 1])
            build(k, number % 2, late)
            late = collect(number % 2, sources[number])
        for piece in late:
            piece()
    else:
        for i in range(ns):
            stack[i] = sources[i][...]

        def step(i, _):
            source = stack.at[i]
            measure(0, source)
            for piece in match(0, source):
                piece()
            build(numbers[0] + i, 0)
            for piece in collect(0, source):
                piece()
            return 0

        lax.fori_loop(0, ns, step, 0)
    for t in range(count):
        out[t][...] = total[t]


def join_kernel(*refs):
    total = refs[0][...]
    for piece in refs[1:-1]:
        total = total + piece[...]
    refs[-1][...] = total


def finish_kernel(*refs, nr):
    emissivity, emission = refs[0:2]
    pieces = refs[2 : 2 + nr]
    radiosity_out, adjoint_out, gradient = refs[2 + nr :]
    cases = emission.shape[0]
    total = pieces[0][...]
    for piece in pieces[1:]:
        total = total + piece[...]
    incoming = total[0:cases]
    returned = total[cases:]
    mine = emissivity[...]
    power = emission[...]
    radiosity_out[...] = mine * power + (1.0 - mine) * incoming
    adjoint_out[...] = returned
    gradient[...] = jnp.sum(returned * (power - incoming), axis=0, keepdims=True)


def busy(micros):
    return pl.CostEstimate(flops=int(micros * 1.1e9), bytes_accessed=0, transcendentals=0)


def swap(x, axis, other):
    if other == 0:
        return x
    return lax.ppermute(x, axis, [(i, i ^ other) for i in range(lax.axis_size(axis))])


def local(
    positions,
    angles,
    areas,
    emissivity,
    emission,
    radiosity_in,
    adjoint_in,
    visibility,
    inlet_patches,
    inlet_weights,
):
    nz = lax.axis_size("emit")
    nr = lax.axis_size("recv")
    own = areas.shape[0]
    cases = emission.shape[0]
    per = own // BLK
    ids = inlet_patches.reshape(1, -1)
    vmem = pl.BlockSpec(memory_space=pltpu.VMEM)
    hbm = pl.BlockSpec(memory_space=pltpu.HBM)
    small = pltpu.CompilerParams(vmem_limit_bytes=4 << 20)
    f32 = jnp.float32
    blocks = nr * per
    rows = 2 * cases + GEO + blocks
    given = (
        positions,
        angles,
        areas.reshape(1, own),
        emissivity.reshape(1, own),
        radiosity_in,
        adjoint_in,
        emission,
        ids,
        inlet_weights,
    )
    given = tuple(pltpu.with_memory_space_constraint(x, pltpu.HBM) for x in given)
    seen = pltpu.with_memory_space_constraint(visibility, pltpu.HBM)
    packed = pl.pallas_call(
        functools.partial(pack_kernel, nr=nr, nz=nz, held=len(given)),
        out_shape=(jax.ShapeDtypeStruct((SLAB, own), jnp.bfloat16),)
        + (jax.ShapeDtypeStruct((rows, own), jnp.bfloat16),) * nz
        + tuple(jax.ShapeDtypeStruct(given[i].shape, given[i].dtype) for i in (3, 6, 7, 8))
        + (jax.ShapeDtypeStruct((nz * blocks, own), f32),),
        in_specs=[hbm] * (1 + len(given)),
        out_specs=(vmem,) * (1 + nz + 5),
        scratch_shapes=[
            pltpu.VMEM((3, own), f32),
            pltpu.VMEM((2, own), f32),
            pltpu.VMEM((1, own), f32),
            pltpu.VMEM((cases, own), f32),
            pltpu.VMEM((cases, own), f32),
            pltpu.VMEM((nz, GEO + blocks, own), f32),
            pltpu.SMEM(visibility.shape, jnp.int32),
            pltpu.SemaphoreType.DMA((len(given),)),
            pltpu.SemaphoreType.DMA,
        ],
        compiler_params=small,
    )(seen, *given)
    mine, power, ids, weights, mask = packed[1 + nz :]
    targets = []
    for s in range(nr):
        targets.append(swap(targets[s - 1], "recv", 1) if s % 2 else swap(packed[0], "recv", s))
    sources = [swap(packed[1 + k], "emit", k) for k in range(nz)]
    source = pl.pallas_call(
        source_kernel,
        out_shape=jax.ShapeDtypeStruct((2 * cases, own), f32),
        in_specs=[vmem] * 2,
        out_specs=vmem,
        compiler_params=small,
        cost_estimate=busy(0.5),
    )(ids, weights)
    pick = jnp.asarray(selection(), jnp.bfloat16)
    sums = jax.ShapeDtypeStruct((2 * cases, own), f32)
    zero = jnp.zeros((2 * cases, own), f32)

    left_kind = jax.ShapeDtypeStruct((own, 2 * FEAT), jnp.bfloat16)
    wide_kind = jax.ShapeDtypeStruct((own, 4 * BLK), f32)

    def prepare(chosen):
        count = len(chosen)
        made = pl.pallas_call(
            functools.partial(prepare_kernel, count=count),
            out_shape=(left_kind,) * count + (wide_kind,) * count,
            in_specs=[vmem] * (1 + count),
            out_specs=(vmem,) * (2 * count),
            compiler_params=pltpu.CompilerParams(vmem_limit_bytes=(2 + 3 * count) << 20),
            cost_estimate=busy(0.2 * count),
        )(pick, *chosen)
        return list(zip(made[:count], made[count:]))

    def add(slots, numbers, begin):
        count, ns = len(slots), len(numbers)
        return list(
            pl.pallas_call(
                functools.partial(sum_kernel, slots=slots, blocks=blocks, numbers=numbers),
                out_shape=(sums,) * count,
                in_specs=[vmem] * (1 + 3 * count + ns),
                out_specs=(vmem,) * count,
                scratch_shapes=[
                    *[pltpu.VMEM((count * own, own), f32)] * 4,
                    *[pltpu.VMEM((count * own, own), jnp.bfloat16)] * 4,
                    pltpu.VMEM((count, 2 * cases, own), f32),
                    pltpu.VMEM((ns if ns > 4 else 1, rows, own), jnp.bfloat16),
                    pltpu.VMEM((2, 8, own), f32),
                    pltpu.VMEM((2, blocks, own), f32),
                ],
                compiler_params=pltpu.CompilerParams(vmem_limit_bytes=12 << 20),
                cost_estimate=busy(0.3 * count * ns),
            )(
                mask,
                *[shapes[t][0] for t in slots],
                *[shapes[t][1] for t in slots],
                *[sources[k] for k in numbers],
                *begin,
            )
        )

    shapes = prepare(targets[:2]) + prepare(targets[2:])
    rest = tuple(range(1, nz))
    begun = []
    for first in range(0, nr, 2):
        begun += add((first, first + 1), (0,), [zero if first else source, zero])
    far_sums = []
    for first in range(2, nr, 2):
        far_sums += add((first, first + 1), rest, begun[first : first + 2])
    far_sums, near_sums = lax.optimization_barrier((far_sums, begun[:2]))
    near_sums = add((0, 1), rest, near_sums)
    far = pl.pallas_call(
        join_kernel,
        out_shape=sums,
        in_specs=[vmem] * (nr - 2),
        out_specs=vmem,
        compiler_params=small,
        cost_estimate=busy(8.0),
    )(*[swap(x, "recv", s + 2) for s, x in enumerate(far_sums)])
    pieces = [far, near_sums[0], swap(near_sums[1], "recv", 1)]
    whole = jax.ShapeDtypeStruct((cases, own), f32)
    radiosity_out, adjoint_out, gradient = pl.pallas_call(
        functools.partial(finish_kernel, nr=len(pieces)),
        out_shape=(whole, whole, jax.ShapeDtypeStruct((1, own), f32)),
        in_specs=[vmem] * (2 + len(pieces)),
        out_specs=(vmem, vmem, vmem),
        compiler_params=small,
    )(mine, power, *pieces)
    return radiosity_out, adjoint_out, gradient.reshape(own)


def solution(mesh):
    patch = ("groups", "emit", "recv")
    placed = (
        P(None, patch),
        P(None, patch),
        P(patch),
        P(patch),
        P(None, patch),
        P(None, patch),
        P(None, patch),
        P(("groups", "emit"), None),
        P("groups"),
        P(None, "groups"),
    )
    return jax.shard_map(
        local,
        mesh=mesh,
        in_specs=placed,
        out_specs=(P(None, patch), P(None, patch), P(patch)),
        check_vma=False,
    )
```

```python
import functools
import math

import jax
import jax.numpy as jnp
import numpy as np
from jax import lax
from jax.experimental import pallas as pl
from jax.experimental.pallas import tpu as pltpu
from jax.sharding import PartitionSpec as P

BLK = 128
GEO = 24
SLAB = 32
FEAT = 128
ROWS = 32
NT = (((1,), (1,)), ((), ()))
TN = (((0,), (0,)), ((), ()))


def selection():
    pick = np.zeros((SLAB, 2 * FEAT + 4 * BLK), np.float32)
    for part in range(3):
        base = part * SLAB
        for split in range(3):
            for axis in range(3):
                pick[9 + 3 * part + axis, base + 3 * split + axis] = 1.0
                pick[3 * part + axis, FEAT + base + 9 + 3 * split + axis] = 1.0
        pick[18 + part, 3 * SLAB + part] = 1.0
        pick[24, FEAT + 18 + part] = 1.0
        for axis in range(3):
            first = 2 * FEAT + axis * BLK
            pick[3 * part + axis, first : first + BLK] = 1.0
        first = 2 * FEAT + 3 * BLK
        pick[21 + part, first : first + BLK] = 1.0
    return pick


def parts(x):
    high = x.astype(jnp.bfloat16).astype(jnp.float32)
    rest = x - high
    middle = rest.astype(jnp.bfloat16).astype(jnp.float32)
    return high, middle, rest - middle


def pack_kernel(*refs, nr, nz, held):
    given = refs[1 : 1 + held]
    target_ref = refs[1 + held]
    sources = refs[2 + held : 2 + held + nz]
    kept = refs[2 + held + nz : 2 + held + nz + 5]
    mask_ref = refs[2 + held + nz + 5]
    place_ref, turn_ref, area_ref, radiosity, adjoint, geo, seen, sems, seen_sem = refs[2 + held + nz + 6 :]
    emissivity_ref = kept[0]
    landing = (place_ref, turn_ref, area_ref, emissivity_ref, radiosity, adjoint) + tuple(kept[1:])
    copies = [pltpu.make_async_copy(a, b, sems.at[i]) for i, (a, b) in enumerate(zip(given, landing))]
    sight = pltpu.make_async_copy(refs[0], seen, seen_sem)
    sight.start()
    for copy in copies:
        copy.start()
    me_r = lax.axis_index("recv")
    me_z = lax.axis_index("emit")
    own = area_ref.shape[1]
    cases = radiosity.shape[0]
    per = own // BLK
    for copy in copies[:3]:
        copy.wait()
    place = place_ref[...]
    turn = turn_ref[...]
    sines = jnp.sin(turn)
    cosines = jnp.cos(turn)
    normal = jnp.concatenate(
        [sines[0:1] * cosines[1:2], sines[0:1] * sines[1:2], cosines[0:1]], axis=0
    )
    product = normal * place
    offset = -(product[0:1] + product[1:2] + product[2:3])
    for number, (a, b, c, d) in enumerate(
        zip(parts(place), parts(normal), parts(offset), parts(area_ref[...]))
    ):
        geo[0, 3 * number : 3 * number + 3, :] = a
        geo[0, 9 + 3 * number : 12 + 3 * number, :] = b
        geo[0, 18 + number : 19 + number, :] = c
        geo[0, 21 + number : 22 + number, :] = d
    sight.wait()
    for k in range(nz):
        for s in range(nr):
            for ib in range(per):
                row = GEO + s * per + ib
                col = ((me_z ^ k) * nr + (me_r ^ s)) * per + ib
                spot = (k * nr + s) * per + ib
                for jb in range(per):
                    lanes = slice(jb * BLK, (jb + 1) * BLK)
                    sees = seen[me_r * per + jb, col].astype(jnp.float32)
                    geo[k, row : row + 1, lanes] = jnp.full((1, BLK), sees, jnp.float32)
                    other = seen[(me_r ^ s) * per + ib, ((me_z ^ k) * nr + me_r) * per + jb]
                    sees = other.astype(jnp.float32) * (1.0 / math.pi)
                    mask_ref[spot : spot + 1, lanes] = jnp.full((1, BLK), sees, jnp.float32)
    shared = geo[0, 0:GEO, :]
    one = jnp.ones((SLAB - GEO, own), jnp.float32)
    target_ref[...] = jnp.concatenate([shared, one], axis=0).astype(jnp.bfloat16)
    for copy in copies[3:6]:
        copy.wait()
    value = radiosity[...].astype(jnp.bfloat16)
    weighted = ((1.0 - emissivity_ref[...]) * adjoint[...]).astype(jnp.bfloat16)
    for k in range(nz):
        sources[k][0:cases, :] = value
        sources[k][cases : 2 * cases, :] = weighted
        sources[k][2 * cases :, :] = jnp.concatenate([shared, geo[k, GEO:, :]], axis=0).astype(jnp.bfloat16)
    for copy in copies[6:]:
        copy.wait()


def source_kernel(ids, weights, out_ref):
    own = out_ref.shape[1]
    first = (lax.axis_index("emit") * lax.axis_size("recv") + lax.axis_index("recv")) * own
    half = out_ref.shape[0] // 2
    hit = lax.broadcasted_iota(jnp.int32, (own, ids.shape[1]), 0) == ids[...] - first
    chosen = jnp.where(hit, 1.0, 0.0).astype(jnp.bfloat16)
    pieces = jnp.concatenate(parts(weights[...]), axis=0).astype(jnp.bfloat16)
    split = lax.dot_general(pieces, chosen, NT, preferred_element_type=jnp.float32)
    out_ref[0:half, :] = jnp.zeros((half, own), jnp.float32)
    out_ref[half:, :] = split[0:half] + split[half : 2 * half] + split[2 * half :]


def one_row(ref, row, lanes):
    if isinstance(row, int):
        return ref[row : row + 1, lanes]
    around = ref[pl.ds(pl.multiple_of(row // 8 * 8, 8), 8), lanes]
    pick = lax.broadcasted_iota(jnp.int32, around.shape, 0) == row % 8
    return jnp.sum(jnp.where(pick, around, 0.0), axis=0, keepdims=True)


def prepare_kernel(*refs, count):
    pick = refs[0]
    targets = refs[1 : 1 + count]
    left = refs[1 + count : 1 + 2 * count]
    wide = refs[1 + 2 * count :]
    own = targets[0].shape[1]
    both = jnp.concatenate([target[...] for target in targets], axis=1)
    feature = lax.dot_general(both, pick[...], TN, preferred_element_type=jnp.float32)
    for t in range(count):
        lines = slice(t * own, (t + 1) * own)
        left[t][...] = feature[lines, : 2 * FEAT].astype(jnp.bfloat16)
        wide[t][...] = feature[lines, 2 * FEAT :]


def sum_kernel(*refs, slots, blocks, numbers):
    ns, count = len(numbers), len(slots)
    refs = list(refs)

    def take(amount):
        taken = refs[:amount]
        del refs[:amount]
        return taken

    mask = take(1)[0]
    left, wide = take(count), take(count)
    sources = take(ns)
    begin, out = take(count), take(count)
    facing, back, fwd_tile, adj_tile = take(2), take(2), take(2), take(2)
    total, stack, geo, scale_q = refs
    own = out[0].shape[1]
    cases = out[0].shape[0] // 2
    per = own // BLK
    for t in range(count):
        total[t] = begin[t][...]

    def match(slot, source):
        slab = source[2 * cases : 2 * cases + SLAB, :]
        right = jnp.concatenate([slab, slab, slab, jnp.ones_like(slab)], axis=0)

        def piece(t, which):
            cols = slice(FEAT, 2 * FEAT) if which else slice(0, FEAT)
            (back if which else facing)[slot][t * own : (t + 1) * own, :] = jnp.dot(
                left[t][:, cols], right, preferred_element_type=jnp.float32
            )

        return [functools.partial(piece, t, which) for t in range(count) for which in (0, 1)]

    def measure(slot, source):
        exact = source[2 * cases :, :].astype(jnp.float32)
        geo[slot, 0:3, :] = exact[0:3] + exact[3:6] + exact[6:9]
        area_q = exact[21:22] + exact[22:23] + exact[23:24]
        geo[slot, 3:4, :] = area_q
        scale_q[slot] = exact[GEO:] * (area_q * (1.0 / math.pi))

    def build(k, slot, woven=()):
        spots, spot = count * own // ROWS, 0
        amount, done = len(woven), 0
        marks = []
        for jb in range(per):
            lanes = slice(jb * BLK, (jb + 1) * BLK)
            marks.append((lanes, [geo[slot, c : c + 1, lanes] for c in range(4)]))
        for t in range(count):
            for ib in range(per):
                row = slots[t] * per + ib
                pairs = [
                    (lanes, place, one_row(scale_q.at[slot], row, lanes), one_row(mask, k * blocks + row, lanes))
                    for lanes, place in marks
                ]
                for start in range(ib * BLK, (ib + 1) * BLK, ROWS):
                    here = slice(start, start + ROWS)
                    there = slice(t * own + start, t * own + start + ROWS)
                    x, y, z, area = (wide[t][here, c * BLK : (c + 1) * BLK] for c in range(4))
                    for lanes, (xq, yq, zq, aq), scale, sees in pairs:
                        dx = x - xq
                        dy = y - yq
                        dz = z - zq
                        square = dx * dx + dy * dy + dz * dz
                        faced = jnp.maximum(facing[slot][there, lanes], 0.0)
                        product = faced * jnp.maximum(back[slot][there, lanes], 0.0)
                        near = square + aq
                        far = square + area
                        fwd_tile[slot][there, lanes] = (product * scale / (near * near)).astype(jnp.bfloat16)
                        adj_tile[slot][there, lanes] = (product * sees * area / (far * far)).astype(jnp.bfloat16)
                    spot += 1
                    due = spot * amount // spots
                    while done < due:
                        woven[done]()
                        done += 1

    def collect(slot, source):
        def piece(t, which):
            lines = slice(cases, 2 * cases) if which else slice(0, cases)
            tile = (adj_tile if which else fwd_tile)[slot][t * own : (t + 1) * own, :]
            total[t, lines, :] += lax.dot_general(source[lines, :], tile, NT, preferred_element_type=jnp.float32)

        return [functools.partial(piece, t, which) for t in range(count) for which in (0, 1)]

    if ns <= 4:
        late = []
        for number, k in enumerate(numbers):
            if number == 0:
                measure(0, sources[0])
                for piece in match(0, sources[0]):
                    piece()
            if number + 1 < ns:
                measure((number + 1) % 2, sources[number + 1])
                late = late + match((number + 1) % 2, sources[number + 1])
            build(k, number % 2, late)
            late = collect(number % 2, sources[number])
        for piece in late:
            piece()
    else:
        for i in range(ns):
            stack[i] = sources[i][...]

        def step(i, _):
            source = stack.at[i]
            measure(0, source)
            for piece in match(0, source):
                piece()
            build(numbers[0] + i * (numbers[1] - numbers[0]), 0)
            for piece in collect(0, source):
                piece()
            return 0

        lax.fori_loop(0, ns, step, 0)
    for t in range(count):
        out[t][...] = total[t]


def join_kernel(*refs):
    total = refs[0][...]
    for piece in refs[1:-1]:
        total = total + piece[...]
    refs[-1][...] = total


def finish_kernel(*refs, nr):
    emissivity, emission = refs[0:2]
    pieces = refs[2 : 2 + nr]
    radiosity_out, adjoint_out, gradient = refs[2 + nr :]
    cases = emission.shape[0]
    total = pieces[0][...]
    for piece in pieces[1:]:
        total = total + piece[...]
    incoming = total[0:cases]
    returned = total[cases:]
    mine = emissivity[...]
    power = emission[...]
    radiosity_out[...] = mine * power + (1.0 - mine) * incoming
    adjoint_out[...] = returned
    gradient[...] = jnp.sum(returned * (power - incoming), axis=0, keepdims=True)


def busy(micros):
    return pl.CostEstimate(flops=int(micros * 1.1e9), bytes_accessed=0, transcendentals=0)


def swap(x, axis, other):
    if other == 0:
        return x
    return lax.ppermute(x, axis, [(i, i ^ other) for i in range(lax.axis_size(axis))])


def local(
    positions,
    angles,
    areas,
    emissivity,
    emission,
    radiosity_in,
    adjoint_in,
    visibility,
    inlet_patches,
    inlet_weights,
):
    nz = lax.axis_size("emit")
    nr = lax.axis_size("recv")
    own = areas.shape[0]
    cases = emission.shape[0]
    per = own // BLK
    ids = inlet_patches.reshape(1, -1)
    vmem = pl.BlockSpec(memory_space=pltpu.VMEM)
    hbm = pl.BlockSpec(memory_space=pltpu.HBM)
    small = pltpu.CompilerParams(vmem_limit_bytes=4 << 20)
    f32 = jnp.float32
    blocks = nr * per
    rows = 2 * cases + GEO + blocks
    given = (
        positions,
        angles,
        areas.reshape(1, own),
        emissivity.reshape(1, own),
        radiosity_in,
        adjoint_in,
        emission,
        ids,
        inlet_weights,
        jnp.asarray(selection(), jnp.bfloat16),
    )
    given = tuple(pltpu.with_memory_space_constraint(x, pltpu.HBM) for x in given)
    seen = pltpu.with_memory_space_constraint(visibility, pltpu.HBM)
    packed = pl.pallas_call(
        functools.partial(pack_kernel, nr=nr, nz=nz, held=len(given)),
        out_shape=(jax.ShapeDtypeStruct((SLAB, own), jnp.bfloat16),)
        + (jax.ShapeDtypeStruct((rows, own), jnp.bfloat16),) * nz
        + tuple(jax.ShapeDtypeStruct(given[i].shape, given[i].dtype) for i in (3, 6, 7, 8, 9))
        + (jax.ShapeDtypeStruct((nz * blocks, own), f32),),
        in_specs=[hbm] * (1 + len(given)),
        out_specs=(vmem,) * (1 + nz + 6),
        scratch_shapes=[
            pltpu.VMEM((3, own), f32),
            pltpu.VMEM((2, own), f32),
            pltpu.VMEM((1, own), f32),
            pltpu.VMEM((cases, own), f32),
            pltpu.VMEM((cases, own), f32),
            pltpu.VMEM((nz, GEO + blocks, own), f32),
            pltpu.SMEM(visibility.shape, jnp.int32),
            pltpu.SemaphoreType.DMA((len(given),)),
            pltpu.SemaphoreType.DMA,
        ],
        compiler_params=small,
    )(seen, *given)
    mine, power, ids, weights, pick, mask = packed[1 + nz :]
    targets = []
    for s in range(nr):
        targets.append(swap(targets[s - 1], "recv", 1) if s % 2 else swap(packed[0], "recv", s))
    sources = {k: swap(packed[1 + k], "emit", k) for k in reversed(range(nz))}
    source = pl.pallas_call(
        source_kernel,
        out_shape=jax.ShapeDtypeStruct((2 * cases, own), f32),
        in_specs=[vmem] * 2,
        out_specs=vmem,
        compiler_params=small,
        cost_estimate=busy(0.5),
    )(ids, weights)
    sums = jax.ShapeDtypeStruct((2 * cases, own), f32)
    zero = jnp.zeros((2 * cases, own), f32)

    left_kind = jax.ShapeDtypeStruct((own, 2 * FEAT), jnp.bfloat16)
    wide_kind = jax.ShapeDtypeStruct((own, 4 * BLK), f32)

    def prepare(chosen):
        count = len(chosen)
        made = pl.pallas_call(
            functools.partial(prepare_kernel, count=count),
            out_shape=(left_kind,) * count + (wide_kind,) * count,
            in_specs=[vmem] * (1 + count),
            out_specs=(vmem,) * (2 * count),
            compiler_params=pltpu.CompilerParams(vmem_limit_bytes=(2 + 3 * count) << 20),
            cost_estimate=busy(0.2 * count),
        )(pick, *chosen)
        return list(zip(made[:count], made[count:]))

    def add(slots, numbers, begin):
        count, ns = len(slots), len(numbers)
        return list(
            pl.pallas_call(
                functools.partial(sum_kernel, slots=slots, blocks=blocks, numbers=numbers),
                out_shape=(sums,) * count,
                in_specs=[vmem] * (1 + 3 * count + ns),
                out_specs=(vmem,) * count,
                scratch_shapes=[
                    *[pltpu.VMEM((count * own, own), f32)] * 4,
                    *[pltpu.VMEM((count * own, own), jnp.bfloat16)] * 4,
                    pltpu.VMEM((count, 2 * cases, own), f32),
                    pltpu.VMEM((ns if ns > 4 else 1, rows, own), jnp.bfloat16),
                    pltpu.VMEM((2, 8, own), f32),
                    pltpu.VMEM((2, blocks, own), f32),
                ],
                compiler_params=pltpu.CompilerParams(vmem_limit_bytes=12 << 20),
                cost_estimate=busy(0.3 * count * ns),
            )(
                mask,
                *[shapes[t][0] for t in slots],
                *[shapes[t][1] for t in slots],
                *[sources[k] for k in numbers],
                *begin,
            )
        )

    shapes = prepare(targets[:2]) + prepare(targets[2:])
    rest = tuple(range(nz - 1, 0, -1))
    begun = []
    for first in range(0, nr, 2):
        begun += add((first, first + 1), (0,), [zero if first else source, zero])
    far_sums = []
    for first in range(2, nr, 2):
        far_sums += add((first, first + 1), rest, begun[first : first + 2])
    far_sums, near_sums = lax.optimization_barrier((far_sums, begun[:2]))
    near_sums = add((0, 1), rest, near_sums)
    far = pl.pallas_call(
        join_kernel,
        out_shape=sums,
        in_specs=[vmem] * (nr - 2),
        out_specs=vmem,
        compiler_params=small,
        cost_estimate=busy(8.0),
    )(*[swap(far_sums[s - 2], "recv", s) for s in reversed(range(2, nr))])
    pieces = [far, near_sums[0], swap(near_sums[1], "recv", 1)]
    whole = jax.ShapeDtypeStruct((cases, own), f32)
    radiosity_out, adjoint_out, gradient = pl.pallas_call(
        functools.partial(finish_kernel, nr=len(pieces)),
        out_shape=(whole, whole, jax.ShapeDtypeStruct((1, own), f32)),
        in_specs=[vmem] * (2 + len(pieces)),
        out_specs=(vmem, vmem, vmem),
        compiler_params=small,
    )(mine, power, *pieces)
    return radiosity_out, adjoint_out, gradient.reshape(own)


def solution(mesh):
    patch = ("groups", "emit", "recv")
    placed = (
        P(None, patch),
        P(None, patch),
        P(patch),
        P(patch),
        P(None, patch),
        P(None, patch),
        P(None, patch),
        P(("groups", "emit"), None),
        P("groups"),
        P(None, "groups"),
    )
    return jax.shard_map(
        local,
        mesh=mesh,
        in_specs=placed,
        out_specs=(P(None, patch), P(None, patch), P(patch)),
        check_vma=False,
    )
```

```python
import functools
import math

import jax
import jax.numpy as jnp
import numpy as np
from jax import lax
from jax.experimental import pallas as pl
from jax.experimental.pallas import tpu as pltpu
from jax.sharding import PartitionSpec as P

BLK = 128
GEO = 24
SLAB = 32
FEAT = 128
ROWS = 32
NT = (((1,), (1,)), ((), ()))
TN = (((0,), (0,)), ((), ()))


def selection():
    pick = np.zeros((SLAB, 2 * FEAT + 4 * BLK), np.float32)
    for part in range(3):
        base = part * SLAB
        for split in range(3):
            for axis in range(3):
                pick[9 + 3 * part + axis, base + 3 * split + axis] = 1.0
                pick[3 * part + axis, FEAT + base + 9 + 3 * split + axis] = 1.0
        pick[18 + part, 3 * SLAB + part] = 1.0
        pick[24, FEAT + 18 + part] = 1.0
        for axis in range(3):
            first = 2 * FEAT + axis * BLK
            pick[3 * part + axis, first : first + BLK] = 1.0
        first = 2 * FEAT + 3 * BLK
        pick[21 + part, first : first + BLK] = 1.0
    return pick


def parts(x):
    high = x.astype(jnp.bfloat16).astype(jnp.float32)
    rest = x - high
    middle = rest.astype(jnp.bfloat16).astype(jnp.float32)
    return high, middle, rest - middle


def pack_kernel(*refs, nr, nz, held):
    given = refs[1 : 1 + held]
    target_ref = refs[1 + held]
    sources = refs[2 + held : 2 + held + nz]
    kept = refs[2 + held + nz : 2 + held + nz + 5]
    mask_ref = refs[2 + held + nz + 5]
    place_ref, turn_ref, area_ref, radiosity, adjoint, geo, seen, sems, seen_sem = refs[2 + held + nz + 6 :]
    emissivity_ref = kept[0]
    landing = (place_ref, turn_ref, area_ref, emissivity_ref, radiosity, adjoint) + tuple(kept[1:])
    copies = [pltpu.make_async_copy(a, b, sems.at[i]) for i, (a, b) in enumerate(zip(given, landing))]
    sight = pltpu.make_async_copy(refs[0], seen, seen_sem)
    sight.start()
    for copy in copies:
        copy.start()
    me_r = lax.axis_index("recv")
    me_z = lax.axis_index("emit")
    own = area_ref.shape[1]
    cases = radiosity.shape[0]
    per = own // BLK
    for copy in copies[:3]:
        copy.wait()
    place = place_ref[...]
    turn = turn_ref[...]
    sines = jnp.sin(turn)
    cosines = jnp.cos(turn)
    normal = jnp.concatenate(
        [sines[0:1] * cosines[1:2], sines[0:1] * sines[1:2], cosines[0:1]], axis=0
    )
    product = normal * place
    offset = -(product[0:1] + product[1:2] + product[2:3])
    for number, (a, b, c, d) in enumerate(
        zip(parts(place), parts(normal), parts(offset), parts(area_ref[...]))
    ):
        geo[0, 3 * number : 3 * number + 3, :] = a
        geo[0, 9 + 3 * number : 12 + 3 * number, :] = b
        geo[0, 18 + number : 19 + number, :] = c
        geo[0, 21 + number : 22 + number, :] = d
    sight.wait()
    for k in range(nz):
        for s in range(nr):
            for ib in range(per):
                row = GEO + s * per + ib
                col = ((me_z ^ k) * nr + (me_r ^ s)) * per + ib
                spot = (k * nr + s) * per + ib
                for jb in range(per):
                    lanes = slice(jb * BLK, (jb + 1) * BLK)
                    sees = seen[me_r * per + jb, col].astype(jnp.float32)
                    geo[k, row : row + 1, lanes] = jnp.full((1, BLK), sees, jnp.float32)
                    other = seen[(me_r ^ s) * per + ib, ((me_z ^ k) * nr + me_r) * per + jb]
                    sees = other.astype(jnp.float32) * (1.0 / math.pi)
                    mask_ref[spot : spot + 1, lanes] = jnp.full((1, BLK), sees, jnp.float32)
    shared = geo[0, 0:GEO, :]
    one = jnp.ones((SLAB - GEO, own), jnp.float32)
    target_ref[...] = jnp.concatenate([shared, one], axis=0).astype(jnp.bfloat16)
    for copy in copies[3:6]:
        copy.wait()
    value = radiosity[...].astype(jnp.bfloat16)
    weighted = ((1.0 - emissivity_ref[...]) * adjoint[...]).astype(jnp.bfloat16)
    for k in range(nz):
        sources[k][0:cases, :] = value
        sources[k][cases : 2 * cases, :] = weighted
        sources[k][2 * cases :, :] = jnp.concatenate([shared, geo[k, GEO:, :]], axis=0).astype(jnp.bfloat16)
    for copy in copies[6:]:
        copy.wait()


def source_kernel(ids, weights, out_ref):
    own = out_ref.shape[1]
    first = (lax.axis_index("emit") * lax.axis_size("recv") + lax.axis_index("recv")) * own
    half = out_ref.shape[0] // 2
    hit = lax.broadcasted_iota(jnp.int32, (own, ids.shape[1]), 0) == ids[...] - first
    chosen = jnp.where(hit, 1.0, 0.0).astype(jnp.bfloat16)
    pieces = jnp.concatenate(parts(weights[...]), axis=0).astype(jnp.bfloat16)
    split = lax.dot_general(pieces, chosen, NT, preferred_element_type=jnp.float32)
    out_ref[0:half, :] = jnp.zeros((half, own), jnp.float32)
    out_ref[half:, :] = split[0:half] + split[half : 2 * half] + split[2 * half :]


def one_row(ref, row, lanes):
    if isinstance(row, int):
        return ref[row : row + 1, lanes]
    around = ref[pl.ds(pl.multiple_of(row // 8 * 8, 8), 8), lanes]
    pick = lax.broadcasted_iota(jnp.int32, around.shape, 0) == row % 8
    return jnp.sum(jnp.where(pick, around, 0.0), axis=0, keepdims=True)


def prepare_kernel(*refs, count):
    pick = refs[0]
    targets = refs[1 : 1 + count]
    left = refs[1 + count : 1 + 2 * count]
    wide = refs[1 + 2 * count :]
    own = targets[0].shape[1]
    both = jnp.concatenate([target[...] for target in targets], axis=1)
    feature = lax.dot_general(both, pick[...], TN, preferred_element_type=jnp.float32)
    for t in range(count):
        lines = slice(t * own, (t + 1) * own)
        left[t][...] = feature[lines, : 2 * FEAT].astype(jnp.bfloat16)
        wide[t][...] = feature[lines, 2 * FEAT :]


def sum_kernel(*refs, slots, blocks, numbers):
    ns, count = len(numbers), len(slots)
    refs = list(refs)

    def take(amount):
        taken = refs[:amount]
        del refs[:amount]
        return taken

    mask = take(1)[0]
    left, wide = take(count), take(count)
    sources = take(ns)
    begin, out = take(count), take(count)
    facing, back, fwd_tile, adj_tile = take(2), take(2), take(2), take(2)
    stack, geo, scale_q = refs
    own = out[0].shape[1]
    cases = out[0].shape[0] // 2
    per = own // BLK
    def match(slot, source):
        slab = source[2 * cases : 2 * cases + SLAB, :]
        right = jnp.concatenate([slab, slab, slab, jnp.ones_like(slab)], axis=0)

        def piece(t, which):
            cols = slice(FEAT, 2 * FEAT) if which else slice(0, FEAT)
            (back if which else facing)[slot][t * own : (t + 1) * own, :] = jnp.dot(
                left[t][:, cols], right, preferred_element_type=jnp.float32
            )

        return [functools.partial(piece, t, which) for t in range(count) for which in (0, 1)]

    def measure(slot, source):
        exact = source[2 * cases :, :].astype(jnp.float32)
        geo[slot, 0:3, :] = exact[0:3] + exact[3:6] + exact[6:9]
        area_q = exact[21:22] + exact[22:23] + exact[23:24]
        geo[slot, 3:4, :] = area_q
        scale_q[slot] = exact[GEO:] * (area_q * (1.0 / math.pi))

    def build(k, slot, woven=()):
        spots, spot = count * own // ROWS, 0
        amount, done = len(woven), 0
        marks = []
        for jb in range(per):
            lanes = slice(jb * BLK, (jb + 1) * BLK)
            marks.append((lanes, [geo[slot, c : c + 1, lanes] for c in range(4)]))
        for t in range(count):
            for ib in range(per):
                row = slots[t] * per + ib
                pairs = [
                    (lanes, place, one_row(scale_q.at[slot], row, lanes), one_row(mask, k * blocks + row, lanes))
                    for lanes, place in marks
                ]
                for start in range(ib * BLK, (ib + 1) * BLK, ROWS):
                    here = slice(start, start + ROWS)
                    there = slice(t * own + start, t * own + start + ROWS)
                    x, y, z, area = (wide[t][here, c * BLK : (c + 1) * BLK] for c in range(4))
                    for lanes, (xq, yq, zq, aq), scale, sees in pairs:
                        dx = x - xq
                        dy = y - yq
                        dz = z - zq
                        square = dx * dx + dy * dy + dz * dz
                        faced = jnp.maximum(facing[slot][there, lanes], 0.0)
                        product = faced * jnp.maximum(back[slot][there, lanes], 0.0)
                        near = square + aq
                        far = square + area
                        fwd_tile[slot][there, lanes] = (product * scale / (near * near)).astype(jnp.bfloat16)
                        adj_tile[slot][there, lanes] = (product * sees * area / (far * far)).astype(jnp.bfloat16)
                    spot += 1
                    due = spot * amount // spots
                    while done < due:
                        woven[done]()
                        done += 1

    def collect(slot, source, onto):
        def piece(t, which):
            lines = slice(cases, 2 * cases) if which else slice(0, cases)
            tile = (adj_tile if which else fwd_tile)[slot][t * own : (t + 1) * own, :]
            out[t][lines, :] = onto[t][lines, :] + lax.dot_general(
                source[lines, :], tile, NT, preferred_element_type=jnp.float32
            )

        return [functools.partial(piece, t, which) for t in range(count) for which in (0, 1)]

    if ns <= 4:
        late = []
        for number, k in enumerate(numbers):
            if number == 0:
                measure(0, sources[0])
                for piece in match(0, sources[0]):
                    piece()
            if number + 1 < ns:
                measure((number + 1) % 2, sources[number + 1])
                late = late + match((number + 1) % 2, sources[number + 1])
            build(k, number % 2, late)
            late = collect(number % 2, sources[number], out if number else begin)
        for piece in late:
            piece()
    else:
        for i in range(ns):
            stack[i] = sources[i][...]
        for t in range(count):
            out[t][...] = begin[t][...]

        def step(i, _):
            source = stack.at[i]
            measure(0, source)
            for piece in match(0, source):
                piece()
            build(lax.rem(numbers[0] - 1 + i, ns) + 1, 0)
            for piece in collect(0, source, out):
                piece()
            return 0

        lax.fori_loop(0, ns, step, 0)

def join_kernel(*refs):
    total = refs[0][...]
    for piece in refs[1:-1]:
        total = total + piece[...]
    refs[-1][...] = total


def finish_kernel(*refs, nr):
    emissivity, emission = refs[0:2]
    pieces = refs[2 : 2 + nr]
    radiosity_out, adjoint_out, gradient = refs[2 + nr :]
    cases = emission.shape[0]
    total = pieces[0][...]
    for piece in pieces[1:]:
        total = total + piece[...]
    incoming = total[0:cases]
    returned = total[cases:]
    mine = emissivity[...]
    power = emission[...]
    radiosity_out[...] = mine * power + (1.0 - mine) * incoming
    adjoint_out[...] = returned
    gradient[...] = jnp.sum(returned * (power - incoming), axis=0, keepdims=True)


def busy(micros):
    return pl.CostEstimate(flops=int(micros * 1.1e9), bytes_accessed=0, transcendentals=0)


def swap(x, axis, other):
    if other == 0:
        return x
    return lax.ppermute(x, axis, [(i, i ^ other) for i in range(lax.axis_size(axis))])


def local(
    positions,
    angles,
    areas,
    emissivity,
    emission,
    radiosity_in,
    adjoint_in,
    visibility,
    inlet_patches,
    inlet_weights,
):
    nz = lax.axis_size("emit")
    nr = lax.axis_size("recv")
    own = areas.shape[0]
    cases = emission.shape[0]
    per = own // BLK
    ids = inlet_patches.reshape(1, -1)
    vmem = pl.BlockSpec(memory_space=pltpu.VMEM)
    hbm = pl.BlockSpec(memory_space=pltpu.HBM)
    small = pltpu.CompilerParams(vmem_limit_bytes=4 << 20)
    f32 = jnp.float32
    blocks = nr * per
    rows = 2 * cases + GEO + blocks
    given = (
        positions,
        angles,
        areas.reshape(1, own),
        emissivity.reshape(1, own),
        radiosity_in,
        adjoint_in,
        emission,
        ids,
        inlet_weights,
        jnp.asarray(selection(), jnp.bfloat16),
    )
    given = tuple(pltpu.with_memory_space_constraint(x, pltpu.HBM) for x in given)
    seen = pltpu.with_memory_space_constraint(visibility, pltpu.HBM)
    packed = pl.pallas_call(
        functools.partial(pack_kernel, nr=nr, nz=nz, held=len(given)),
        out_shape=(jax.ShapeDtypeStruct((SLAB, own), jnp.bfloat16),)
        + (jax.ShapeDtypeStruct((rows, own), jnp.bfloat16),) * nz
        + tuple(jax.ShapeDtypeStruct(given[i].shape, given[i].dtype) for i in (3, 6, 7, 8, 9))
        + (jax.ShapeDtypeStruct((nz * blocks, own), f32),),
        in_specs=[hbm] * (1 + len(given)),
        out_specs=(vmem,) * (1 + nz + 6),
        scratch_shapes=[
            pltpu.VMEM((3, own), f32),
            pltpu.VMEM((2, own), f32),
            pltpu.VMEM((1, own), f32),
            pltpu.VMEM((cases, own), f32),
            pltpu.VMEM((cases, own), f32),
            pltpu.VMEM((nz, GEO + blocks, own), f32),
            pltpu.SMEM(visibility.shape, jnp.int32),
            pltpu.SemaphoreType.DMA((len(given),)),
            pltpu.SemaphoreType.DMA,
        ],
        compiler_params=small,
    )(seen, *given)
    mine, power, ids, weights, pick, mask = packed[1 + nz :]
    targets = []
    for s in range(nr):
        targets.append(swap(targets[s - 1], "recv", 1) if s % 2 else swap(packed[0], "recv", s))
    sources = {k: swap(packed[1 + k], "emit", k) for k in reversed(range(nz))}
    source = pl.pallas_call(
        source_kernel,
        out_shape=jax.ShapeDtypeStruct((2 * cases, own), f32),
        in_specs=[vmem] * 2,
        out_specs=vmem,
        compiler_params=small,
        cost_estimate=busy(0.5),
    )(ids, weights)
    sums = jax.ShapeDtypeStruct((2 * cases, own), f32)
    zero = jnp.zeros((2 * cases, own), f32)

    left_kind = jax.ShapeDtypeStruct((own, 2 * FEAT), jnp.bfloat16)
    wide_kind = jax.ShapeDtypeStruct((own, 4 * BLK), f32)

    def prepare(chosen):
        count = len(chosen)
        made = pl.pallas_call(
            functools.partial(prepare_kernel, count=count),
            out_shape=(left_kind,) * count + (wide_kind,) * count,
            in_specs=[vmem] * (1 + count),
            out_specs=(vmem,) * (2 * count),
            compiler_params=pltpu.CompilerParams(vmem_limit_bytes=(2 + 3 * count) << 20),
            cost_estimate=busy(0.2 * count),
        )(pick, *chosen)
        return list(zip(made[:count], made[count:]))

    def add(slots, numbers, begin):
        count, ns = len(slots), len(numbers)
        return list(
            pl.pallas_call(
                functools.partial(sum_kernel, slots=slots, blocks=blocks, numbers=numbers),
                out_shape=(sums,) * count,
                in_specs=[vmem] * (1 + 3 * count + ns),
                out_specs=(vmem,) * count,
                scratch_shapes=[
                    *[pltpu.VMEM((count * own, own), f32)] * 4,
                    *[pltpu.VMEM((count * own, own), jnp.bfloat16)] * 4,
                    pltpu.VMEM((ns if ns > 4 else 1, rows, own), jnp.bfloat16),
                    pltpu.VMEM((2, 8, own), f32),
                    pltpu.VMEM((2, blocks, own), f32),
                ],
                compiler_params=pltpu.CompilerParams(vmem_limit_bytes=12 << 20),
                cost_estimate=busy(0.3 * count * ns),
            )(
                mask,
                *[shapes[t][0] for t in slots],
                *[shapes[t][1] for t in slots],
                *[sources[k] for k in numbers],
                *begin,
            )
        )

    shapes = prepare(targets[:2]) + prepare(targets[2:])
    rest = tuple(range(nz // 2, nz)) + tuple(range(1, nz // 2))
    begun = []
    for first in range(0, nr, 2):
        begun += add((first, first + 1), (0,), [zero if first else source, zero])
    far_sums = []
    for first in range(2, nr, 2):
        far_sums += add((first, first + 1), rest, begun[first : first + 2])
    far_sums, near_sums = lax.optimization_barrier((far_sums, begun[:2]))
    near_sums = add((0, 1), rest, near_sums)
    far = pl.pallas_call(
        join_kernel,
        out_shape=sums,
        in_specs=[vmem] * (nr - 2),
        out_specs=vmem,
        compiler_params=small,
        cost_estimate=busy(8.0),
    )(*[swap(far_sums[s - 2], "recv", s) for s in reversed(range(2, nr))])
    pieces = [far, near_sums[0], swap(near_sums[1], "recv", 1)]
    whole = jax.ShapeDtypeStruct((cases, own), f32)
    radiosity_out, adjoint_out, gradient = pl.pallas_call(
        functools.partial(finish_kernel, nr=len(pieces)),
        out_shape=(whole, whole, jax.ShapeDtypeStruct((1, own), f32)),
        in_specs=[vmem] * (2 + len(pieces)),
        out_specs=(vmem, vmem, vmem),
        compiler_params=small,
    )(mine, power, *pieces)
    return radiosity_out, adjoint_out, gradient.reshape(own)


def solution(mesh):
    patch = ("groups", "emit", "recv")
    placed = (
        P(None, patch),
        P(None, patch),
        P(patch),
        P(patch),
        P(None, patch),
        P(None, patch),
        P(None, patch),
        P(("groups", "emit"), None),
        P("groups"),
        P(None, "groups"),
    )
    return jax.shard_map(
        local,
        mesh=mesh,
        in_specs=placed,
        out_specs=(P(None, patch), P(None, patch), P(patch)),
        check_vma=False,
    )
```

```python
import functools
import math

import jax
import jax.numpy as jnp
import numpy as np
from jax import lax
from jax.experimental import pallas as pl
from jax.experimental.pallas import tpu as pltpu
from jax.sharding import PartitionSpec as P

BLK = 128
GEO = 24
WORD = 20
SLAB = 32
FEAT = 128
ROWS = 32
NT = (((1,), (1,)), ((), ()))
TN = (((0,), (0,)), ((), ()))


def selection():
    pick = np.zeros((SLAB, 2 * FEAT + 4 * BLK), np.float32)
    for part in range(3):
        base = part * SLAB
        for split in range(3):
            for axis in range(3):
                pick[9 + 3 * part + axis, base + 3 * split + axis] = 1.0
                pick[3 * part + axis, FEAT + base + 9 + 3 * split + axis] = 1.0
        pick[18 + part, 3 * SLAB + part] = 1.0
        pick[24, FEAT + 18 + part] = 1.0
        for axis in range(3):
            first = 2 * FEAT + axis * BLK
            pick[3 * part + axis, first : first + BLK] = 1.0
        first = 2 * FEAT + 3 * BLK
        pick[21 + part, first : first + BLK] = 1.0
    return pick


def parts(x):
    high = x.astype(jnp.bfloat16).astype(jnp.float32)
    rest = x - high
    middle = rest.astype(jnp.bfloat16).astype(jnp.float32)
    return high, middle, rest - middle


def pack_kernel(*refs, nr, nz, held):
    given = refs[1 : 1 + held]
    target_ref = refs[1 + held]
    sources = refs[2 + held : 2 + held + nz]
    kept = refs[2 + held + nz : 2 + held + nz + 5]
    mask_ref = refs[2 + held + nz + 5]
    place_ref, turn_ref, area_ref, radiosity, adjoint, geo, seen, sems, seen_sem = refs[2 + held + nz + 6 :]
    emissivity_ref = kept[0]
    landing = (place_ref, turn_ref, area_ref, emissivity_ref, radiosity, adjoint) + tuple(kept[1:])
    copies = [pltpu.make_async_copy(a, b, sems.at[i]) for i, (a, b) in enumerate(zip(given, landing))]
    sight = pltpu.make_async_copy(refs[0], seen, seen_sem)
    sight.start()
    for copy in copies:
        copy.start()
    me_r = lax.axis_index("recv")
    me_z = lax.axis_index("emit")
    own = area_ref.shape[1]
    cases = radiosity.shape[0]
    per = own // BLK
    for copy in copies[:3]:
        copy.wait()
    place = place_ref[...]
    turn = turn_ref[...]
    sines = jnp.sin(turn)
    cosines = jnp.cos(turn)
    normal = jnp.concatenate(
        [sines[0:1] * cosines[1:2], sines[0:1] * sines[1:2], cosines[0:1]], axis=0
    )
    product = normal * place
    offset = -(product[0:1] + product[1:2] + product[2:3])
    for number, (a, b, c, d) in enumerate(
        zip(parts(place), parts(normal), parts(offset), parts(area_ref[...]))
    ):
        geo[0, 3 * number : 3 * number + 3, :] = a
        geo[0, 9 + 3 * number : 12 + 3 * number, :] = b
        geo[0, 18 + number : 19 + number, :] = c
        geo[0, 21 + number : 22 + number, :] = d
    third = geo[0, WORD : WORD + 1, :]
    sight.wait()
    for k in range(nz):
        words = [[0.0] * per for _ in range(geo.shape[1] - GEO + 1)]
        for s in range(nr):
            for ib in range(per):
                block = s * per + ib
                col = ((me_z ^ k) * nr + (me_r ^ s)) * per + ib
                spot = (k * nr + s) * per + ib
                for jb in range(per):
                    lanes = slice(jb * BLK, (jb + 1) * BLK)
                    bit = seen[me_r * per + jb, col].astype(jnp.float32) * float(1 << block % 8)
                    words[block // 8][jb] = words[block // 8][jb] + bit
                    other = seen[(me_r ^ s) * per + ib, ((me_z ^ k) * nr + me_r) * per + jb]
                    sees = other.astype(jnp.float32) * (1.0 / math.pi)
                    mask_ref[spot : spot + 1, lanes] = jnp.full((1, BLK), sees, jnp.float32)
        for number in range(-(-nr * per // 8)):
            row = WORD if nr * per <= 8 else GEO + number
            for jb in range(per):
                geo[k, row : row + 1, jb * BLK : (jb + 1) * BLK] = jnp.full((1, BLK), words[number][jb], jnp.float32)
    word = geo[0, WORD : WORD + 1, :]
    geo[0, WORD : WORD + 1, :] = third
    shared = geo[0, 0:GEO, :]
    one = jnp.ones((SLAB - GEO, own), jnp.float32)
    target_ref[...] = jnp.concatenate([shared, one], axis=0).astype(jnp.bfloat16)
    for copy in copies[3:6]:
        copy.wait()
    value = radiosity[...].astype(jnp.bfloat16)
    weighted = ((1.0 - emissivity_ref[...]) * adjoint[...]).astype(jnp.bfloat16)
    for k in range(nz):
        sources[k][0:cases, :] = value
        sources[k][cases : 2 * cases, :] = weighted
        slab = shared
        if nr * per <= 8:
            line = lax.broadcasted_iota(jnp.int32, shared.shape, 0)
            slab = jnp.where(line == WORD, geo[k, WORD : WORD + 1, :] if k else word, shared)
        else:
            slab = jnp.concatenate([shared, geo[k, GEO:, :]], axis=0)
        sources[k][2 * cases :, :] = slab.astype(jnp.bfloat16)
    for copy in copies[6:]:
        copy.wait()


def source_kernel(ids, weights, out_ref):
    own = out_ref.shape[1]
    first = (lax.axis_index("emit") * lax.axis_size("recv") + lax.axis_index("recv")) * own
    half = out_ref.shape[0] // 2
    hit = lax.broadcasted_iota(jnp.int32, (own, ids.shape[1]), 0) == ids[...] - first
    chosen = jnp.where(hit, 1.0, 0.0).astype(jnp.bfloat16)
    pieces = jnp.concatenate(parts(weights[...]), axis=0).astype(jnp.bfloat16)
    split = lax.dot_general(pieces, chosen, NT, preferred_element_type=jnp.float32)
    out_ref[0:half, :] = jnp.zeros((half, own), jnp.float32)
    out_ref[half:, :] = split[0:half] + split[half : 2 * half] + split[2 * half :]


def one_row(ref, row, lanes):
    if isinstance(row, int):
        return ref[row : row + 1, lanes]
    around = ref[pl.ds(pl.multiple_of(row // 8 * 8, 8), 8), lanes]
    pick = lax.broadcasted_iota(jnp.int32, around.shape, 0) == row % 8
    return jnp.sum(jnp.where(pick, around, 0.0), axis=0, keepdims=True)


def prepare_kernel(*refs, count):
    pick = refs[0]
    targets = refs[1 : 1 + count]
    left = refs[1 + count : 1 + 2 * count]
    wide = refs[1 + 2 * count :]
    own = targets[0].shape[1]
    both = jnp.concatenate([target[...] for target in targets], axis=1)
    feature = lax.dot_general(both, pick[...], TN, preferred_element_type=jnp.float32)
    for t in range(count):
        lines = slice(t * own, (t + 1) * own)
        left[t][...] = feature[lines, : 2 * FEAT].astype(jnp.bfloat16)
        wide[t][...] = feature[lines, 2 * FEAT :]


def sum_kernel(*refs, slots, blocks, numbers):
    ns, count = len(numbers), len(slots)
    refs = list(refs)

    def take(amount):
        taken = refs[:amount]
        del refs[:amount]
        return taken

    mask = take(1)[0]
    left, wide = take(count), take(count)
    sources = take(ns)
    begin, out = take(count), take(count)
    facing, back, fwd_tile, adj_tile = take(2), take(2), take(2), take(2)
    stack, geo, slabs, scale_q = refs
    own = out[0].shape[1]
    cases = out[0].shape[0] // 2
    per = own // BLK
    def match(slot, source):
        slab = slabs[slot, :, :].astype(jnp.bfloat16)
        right = jnp.concatenate([slab, slab, slab, jnp.ones_like(slab)], axis=0)

        def piece(t, which):
            cols = slice(FEAT, 2 * FEAT) if which else slice(0, FEAT)
            (back if which else facing)[slot][t * own : (t + 1) * own, :] = jnp.dot(
                left[t][:, cols], right, preferred_element_type=jnp.float32
            )

        return [functools.partial(piece, t, which) for t in range(count) for which in (0, 1)]

    def measure(slot, source):
        exact = source[2 * cases :, :].astype(jnp.float32)
        geo[slot, 0:3, :] = exact[0:3] + exact[3:6] + exact[6:9]
        area_q = exact[21:22] + exact[22:23] + exact[23:24]
        geo[slot, 3:4, :] = area_q
        flow = (exact[9:12] + exact[12:15] + exact[15:18]) * geo[slot, 0:3, :]
        offset = -(flow[0:1] + flow[1:2] + flow[2:3])
        slabs[slot, 0:GEO, :] = exact[0:GEO]
        slabs[slot, GEO:, :] = jnp.zeros((SLAB - GEO, own), jnp.float32)
        slabs[slot, WORD : WORD + 1, :] = offset - exact[18:19] - exact[19:20]
        scaled = area_q * (1.0 / math.pi)
        for number in range(-(-blocks // 8)):
            row = WORD if blocks <= 8 else GEO + number
            bits = min(8, blocks - 8 * number)
            power = jnp.exp2(-lax.broadcasted_iota(jnp.int32, (bits, own), 0).astype(jnp.float32))
            half = jnp.floor((exact[row : row + 1] + 0.5) * power)
            scale_q[slot, 8 * number : 8 * number + bits, :] = (half - 2.0 * jnp.floor(half * 0.5)) * scaled

    def build(k, slot, woven=()):
        spots, spot = count * own // ROWS, 0
        amount, done = len(woven), 0
        marks = []
        for jb in range(per):
            lanes = slice(jb * BLK, (jb + 1) * BLK)
            marks.append((lanes, [geo[slot, c : c + 1, lanes] for c in range(4)]))
        for t in range(count):
            for ib in range(per):
                row = slots[t] * per + ib
                pairs = [
                    (lanes, place, one_row(scale_q.at[slot], row, lanes), one_row(mask, k * blocks + row, lanes))
                    for lanes, place in marks
                ]
                for start in range(ib * BLK, (ib + 1) * BLK, ROWS):
                    here = slice(start, start + ROWS)
                    there = slice(t * own + start, t * own + start + ROWS)
                    x, y, z, area = (wide[t][here, c * BLK : (c + 1) * BLK] for c in range(4))
                    for lanes, (xq, yq, zq, aq), scale, sees in pairs:
                        dx = x - xq
                        dy = y - yq
                        dz = z - zq
                        square = dx * dx + dy * dy + dz * dz
                        faced = jnp.maximum(facing[slot][there, lanes], 0.0)
                        product = faced * jnp.maximum(back[slot][there, lanes], 0.0)
                        near = square + aq
                        far = square + area
                        fwd_tile[slot][there, lanes] = (product * scale / (near * near)).astype(jnp.bfloat16)
                        adj_tile[slot][there, lanes] = (product * sees * area / (far * far)).astype(jnp.bfloat16)
                    spot += 1
                    due = spot * amount // spots
                    while done < due:
                        woven[done]()
                        done += 1

    def collect(slot, source, onto):
        def piece(t, which):
            lines = slice(cases, 2 * cases) if which else slice(0, cases)
            tile = (adj_tile if which else fwd_tile)[slot][t * own : (t + 1) * own, :]
            out[t][lines, :] = onto[t][lines, :] + lax.dot_general(
                source[lines, :], tile, NT, preferred_element_type=jnp.float32
            )

        return [functools.partial(piece, t, which) for t in range(count) for which in (0, 1)]

    if ns <= 4:
        late = []
        for number, k in enumerate(numbers):
            if number == 0:
                measure(0, sources[0])
                for piece in match(0, sources[0]):
                    piece()
            if number + 1 < ns:
                measure((number + 1) % 2, sources[number + 1])
                late = late + match((number + 1) % 2, sources[number + 1])
            build(k, number % 2, late)
            late = collect(number % 2, sources[number], out if number else begin)
        for piece in late:
            piece()
    else:
        for i in range(ns):
            stack[i] = sources[i][...]
        for t in range(count):
            out[t][...] = begin[t][...]

        def step(i, _):
            source = stack.at[i]
            measure(0, source)
            for piece in match(0, source):
                piece()
            build(lax.rem(numbers[0] - 1 + i, ns) + 1, 0)
            for piece in collect(0, source, out):
                piece()
            return 0

        lax.fori_loop(0, ns, step, 0)

def join_kernel(*refs):
    total = refs[0][...]
    for piece in refs[1:-1]:
        total = total + piece[...]
    refs[-1][...] = total


def finish_kernel(*refs, nr):
    emissivity, emission = refs[0:2]
    pieces = refs[2 : 2 + nr]
    radiosity_out, adjoint_out, gradient = refs[2 + nr :]
    cases = emission.shape[0]
    total = pieces[0][...]
    for piece in pieces[1:]:
        total = total + piece[...]
    incoming = total[0:cases]
    returned = total[cases:]
    mine = emissivity[...]
    power = emission[...]
    radiosity_out[...] = mine * power + (1.0 - mine) * incoming
    adjoint_out[...] = returned
    gradient[...] = jnp.sum(returned * (power - incoming), axis=0, keepdims=True)


def busy(micros):
    return pl.CostEstimate(flops=int(micros * 1.1e9), bytes_accessed=0, transcendentals=0)


def swap(x, axis, other):
    if other == 0:
        return x
    return lax.ppermute(x, axis, [(i, i ^ other) for i in range(lax.axis_size(axis))])


def local(
    positions,
    angles,
    areas,
    emissivity,
    emission,
    radiosity_in,
    adjoint_in,
    visibility,
    inlet_patches,
    inlet_weights,
):
    nz = lax.axis_size("emit")
    nr = lax.axis_size("recv")
    own = areas.shape[0]
    cases = emission.shape[0]
    per = own // BLK
    ids = inlet_patches.reshape(1, -1)
    vmem = pl.BlockSpec(memory_space=pltpu.VMEM)
    hbm = pl.BlockSpec(memory_space=pltpu.HBM)
    small = pltpu.CompilerParams(vmem_limit_bytes=4 << 20)
    f32 = jnp.float32
    blocks = nr * per
    extra = 0 if blocks <= 8 else -(-blocks // 64) * 8
    rows = 2 * cases + GEO + extra
    given = (
        positions,
        angles,
        areas.reshape(1, own),
        emissivity.reshape(1, own),
        radiosity_in,
        adjoint_in,
        emission,
        ids,
        inlet_weights,
        jnp.asarray(selection(), jnp.bfloat16),
    )
    given = tuple(pltpu.with_memory_space_constraint(x, pltpu.HBM) for x in given)
    seen = pltpu.with_memory_space_constraint(visibility, pltpu.HBM)
    packed = pl.pallas_call(
        functools.partial(pack_kernel, nr=nr, nz=nz, held=len(given)),
        out_shape=(jax.ShapeDtypeStruct((SLAB, own), jnp.bfloat16),)
        + (jax.ShapeDtypeStruct((rows, own), jnp.bfloat16),) * nz
        + tuple(jax.ShapeDtypeStruct(given[i].shape, given[i].dtype) for i in (3, 6, 7, 8, 9))
        + (jax.ShapeDtypeStruct((nz * blocks, own), f32),),
        in_specs=[hbm] * (1 + len(given)),
        out_specs=(vmem,) * (1 + nz + 6),
        scratch_shapes=[
            pltpu.VMEM((3, own), f32),
            pltpu.VMEM((2, own), f32),
            pltpu.VMEM((1, own), f32),
            pltpu.VMEM((cases, own), f32),
            pltpu.VMEM((cases, own), f32),
            pltpu.VMEM((nz, GEO + extra, own), f32),
            pltpu.SMEM(visibility.shape, jnp.int32),
            pltpu.SemaphoreType.DMA((len(given),)),
            pltpu.SemaphoreType.DMA,
        ],
        compiler_params=small,
    )(seen, *given)
    mine, power, ids, weights, pick, mask = packed[1 + nz :]
    targets = []
    for s in range(nr):
        targets.append(swap(targets[s - 1], "recv", 1) if s % 2 else swap(packed[0], "recv", s))
    sources = {k: swap(packed[1 + k], "emit", k) for k in reversed(range(nz))}
    source = pl.pallas_call(
        source_kernel,
        out_shape=jax.ShapeDtypeStruct((2 * cases, own), f32),
        in_specs=[vmem] * 2,
        out_specs=vmem,
        compiler_params=small,
        cost_estimate=busy(0.5),
    )(ids, weights)
    sums = jax.ShapeDtypeStruct((2 * cases, own), f32)
    zero = jnp.zeros((2 * cases, own), f32)

    left_kind = jax.ShapeDtypeStruct((own, 2 * FEAT), jnp.bfloat16)
    wide_kind = jax.ShapeDtypeStruct((own, 4 * BLK), f32)

    def prepare(chosen):
        count = len(chosen)
        made = pl.pallas_call(
            functools.partial(prepare_kernel, count=count),
            out_shape=(left_kind,) * count + (wide_kind,) * count,
            in_specs=[vmem] * (1 + count),
            out_specs=(vmem,) * (2 * count),
            compiler_params=pltpu.CompilerParams(vmem_limit_bytes=(2 + 3 * count) << 20),
            cost_estimate=busy(0.2 * count),
        )(pick, *chosen)
        return list(zip(made[:count], made[count:]))

    def add(slots, numbers, begin):
        count, ns = len(slots), len(numbers)
        return list(
            pl.pallas_call(
                functools.partial(sum_kernel, slots=slots, blocks=blocks, numbers=numbers),
                out_shape=(sums,) * count,
                in_specs=[vmem] * (1 + 3 * count + ns),
                out_specs=(vmem,) * count,
                scratch_shapes=[
                    *[pltpu.VMEM((count * own, own), f32)] * 4,
                    *[pltpu.VMEM((count * own, own), jnp.bfloat16)] * 4,
                    pltpu.VMEM((ns if ns > 4 else 1, rows, own), jnp.bfloat16),
                    pltpu.VMEM((2, 8, own), f32),
                    pltpu.VMEM((2, SLAB, own), f32),
                    pltpu.VMEM((2, blocks, own), f32),
                ],
                compiler_params=pltpu.CompilerParams(vmem_limit_bytes=12 << 20),
                cost_estimate=busy(0.3 * count * ns),
            )(
                mask,
                *[shapes[t][0] for t in slots],
                *[shapes[t][1] for t in slots],
                *[sources[k] for k in numbers],
                *begin,
            )
        )

    shapes = prepare(targets[:2]) + prepare(targets[2:])
    rest = tuple(range(nz // 2, nz)) + tuple(range(1, nz // 2))
    begun = []
    for first in range(0, nr, 2):
        begun += add((first, first + 1), (0,), [zero if first else source, zero])
    far_sums = []
    for first in range(2, nr, 2):
        far_sums += add((first, first + 1), rest, begun[first : first + 2])
    far_sums, near_sums = lax.optimization_barrier((far_sums, begun[:2]))
    near_sums = add((0, 1), rest, near_sums)
    far = pl.pallas_call(
        join_kernel,
        out_shape=sums,
        in_specs=[vmem] * (nr - 2),
        out_specs=vmem,
        compiler_params=small,
        cost_estimate=busy(8.0),
    )(*[swap(far_sums[s - 2], "recv", s) for s in reversed(range(2, nr))])
    pieces = [far, near_sums[0], swap(near_sums[1], "recv", 1)]
    whole = jax.ShapeDtypeStruct((cases, own), f32)
    radiosity_out, adjoint_out, gradient = pl.pallas_call(
        functools.partial(finish_kernel, nr=len(pieces)),
        out_shape=(whole, whole, jax.ShapeDtypeStruct((1, own), f32)),
        in_specs=[vmem] * (2 + len(pieces)),
        out_specs=(vmem, vmem, vmem),
        compiler_params=small,
    )(mine, power, *pieces)
    return radiosity_out, adjoint_out, gradient.reshape(own)


def solution(mesh):
    patch = ("groups", "emit", "recv")
    placed = (
        P(None, patch),
        P(None, patch),
        P(patch),
        P(patch),
        P(None, patch),
        P(None, patch),
        P(None, patch),
        P(("groups", "emit"), None),
        P("groups"),
        P(None, "groups"),
    )
    return jax.shard_map(
        local,
        mesh=mesh,
        in_specs=placed,
        out_specs=(P(None, patch), P(None, patch), P(patch)),
        check_vma=False,
    )
```

```python
import functools
import math

import jax
import jax.numpy as jnp
import numpy as np
from jax import lax
from jax.experimental import pallas as pl
from jax.experimental.pallas import tpu as pltpu
from jax.sharding import PartitionSpec as P

BLK = 128
GEO = 24
WORD = 20
SLAB = 32
FEAT = 128
ROWS = 32
NT = (((1,), (1,)), ((), ()))
TN = (((0,), (0,)), ((), ()))


def selection():
    pick = np.zeros((SLAB, 2 * FEAT + 4 * BLK), np.float32)
    for part in range(3):
        base = part * SLAB
        for split in range(3):
            for axis in range(3):
                pick[9 + 3 * part + axis, base + 3 * split + axis] = 1.0
                pick[3 * part + axis, FEAT + base + 9 + 3 * split + axis] = 1.0
        pick[18 + part, 3 * SLAB + part] = 1.0
        pick[24, FEAT + 18 + part] = 1.0
        for axis in range(3):
            first = 2 * FEAT + axis * BLK
            pick[3 * part + axis, first : first + BLK] = 1.0
        first = 2 * FEAT + 3 * BLK
        pick[21 + part, first : first + BLK] = 1.0
    return pick


def parts(x):
    high = x.astype(jnp.bfloat16).astype(jnp.float32)
    rest = x - high
    middle = rest.astype(jnp.bfloat16).astype(jnp.float32)
    return high, middle, rest - middle


def pack_kernel(*refs, nr, nz, held):
    given = refs[1 : 1 + held]
    target_ref = refs[1 + held]
    sources = refs[2 + held : 2 + held + nz]
    kept = refs[2 + held + nz : 2 + held + nz + 5]
    mask_ref = refs[2 + held + nz + 5]
    place_ref, turn_ref, area_ref, radiosity, adjoint, geo, seen, sems, seen_sem = refs[2 + held + nz + 6 :]
    emissivity_ref = kept[0]
    landing = (place_ref, turn_ref, area_ref, emissivity_ref, radiosity, adjoint) + tuple(kept[1:])
    copies = [pltpu.make_async_copy(a, b, sems.at[i]) for i, (a, b) in enumerate(zip(given, landing))]
    sight = pltpu.make_async_copy(refs[0], seen, seen_sem)
    sight.start()
    for copy in copies:
        copy.start()
    me_r = lax.axis_index("recv")
    me_z = lax.axis_index("emit")
    own = area_ref.shape[1]
    cases = radiosity.shape[0]
    per = own // BLK
    for copy in copies[:3]:
        copy.wait()
    place = place_ref[...]
    turn = turn_ref[...]
    sines = jnp.sin(turn)
    cosines = jnp.cos(turn)
    normal = jnp.concatenate(
        [sines[0:1] * cosines[1:2], sines[0:1] * sines[1:2], cosines[0:1]], axis=0
    )
    product = normal * place
    offset = -(product[0:1] + product[1:2] + product[2:3])
    for number, (a, b, c, d) in enumerate(
        zip(parts(place), parts(normal), parts(offset), parts(area_ref[...]))
    ):
        geo[0, 3 * number : 3 * number + 3, :] = a
        geo[0, 9 + 3 * number : 12 + 3 * number, :] = b
        geo[0, 18 + number : 19 + number, :] = c
        geo[0, 21 + number : 22 + number, :] = d
    third = geo[0, WORD : WORD + 1, :]
    sight.wait()
    for k in range(nz):
        words = [[0.0] * per for _ in range(geo.shape[1] - GEO + 1)]
        for s in range(nr):
            for ib in range(per):
                block = s * per + ib
                col = ((me_z ^ k) * nr + (me_r ^ s)) * per + ib
                spot = (k * nr + s) * per + ib
                for jb in range(per):
                    lanes = slice(jb * BLK, (jb + 1) * BLK)
                    bit = seen[me_r * per + jb, col].astype(jnp.float32) * float(1 << block % 8)
                    words[block // 8][jb] = words[block // 8][jb] + bit
                    other = seen[(me_r ^ s) * per + ib, ((me_z ^ k) * nr + me_r) * per + jb]
                    sees = other.astype(jnp.float32) * (1.0 / math.pi)
                    mask_ref[spot : spot + 1, lanes] = jnp.full((1, BLK), sees, jnp.float32)
        for number in range(-(-nr * per // 8)):
            row = WORD if nr * per <= 8 else GEO + number
            for jb in range(per):
                geo[k, row : row + 1, jb * BLK : (jb + 1) * BLK] = jnp.full((1, BLK), words[number][jb], jnp.float32)
    word = geo[0, WORD : WORD + 1, :]
    geo[0, WORD : WORD + 1, :] = third
    shared = geo[0, 0:GEO, :]
    one = jnp.ones((SLAB - GEO, own), jnp.float32)
    target_ref[...] = jnp.concatenate([shared, one], axis=0).astype(jnp.bfloat16)
    for copy in copies[3:6]:
        copy.wait()
    value = radiosity[...].astype(jnp.bfloat16)
    weighted = ((1.0 - emissivity_ref[...]) * adjoint[...]).astype(jnp.bfloat16)
    for k in range(nz):
        sources[k][0:cases, :] = value
        sources[k][cases : 2 * cases, :] = weighted
        slab = shared
        if nr * per <= 8:
            line = lax.broadcasted_iota(jnp.int32, shared.shape, 0)
            slab = jnp.where(line == WORD, geo[k, WORD : WORD + 1, :] if k else word, shared)
        else:
            slab = jnp.concatenate([shared, geo[k, GEO:, :]], axis=0)
        sources[k][2 * cases :, :] = slab.astype(jnp.bfloat16)
    for copy in copies[6:]:
        copy.wait()


def source_kernel(ids, weights, out_ref):
    own = out_ref.shape[1]
    first = (lax.axis_index("emit") * lax.axis_size("recv") + lax.axis_index("recv")) * own
    half = out_ref.shape[0] // 2
    hit = lax.broadcasted_iota(jnp.int32, (own, ids.shape[1]), 0) == ids[...] - first
    chosen = jnp.where(hit, 1.0, 0.0).astype(jnp.bfloat16)
    pieces = jnp.concatenate(parts(weights[...]), axis=0).astype(jnp.bfloat16)
    split = lax.dot_general(pieces, chosen, NT, preferred_element_type=jnp.float32)
    out_ref[0:half, :] = jnp.zeros((half, own), jnp.float32)
    out_ref[half:, :] = split[0:half] + split[half : 2 * half] + split[2 * half :]


def one_row(ref, row, lanes):
    if isinstance(row, int):
        return ref[row : row + 1, lanes]
    around = ref[pl.ds(pl.multiple_of(row // 8 * 8, 8), 8), lanes]
    pick = lax.broadcasted_iota(jnp.int32, around.shape, 0) == row % 8
    return jnp.sum(jnp.where(pick, around, 0.0), axis=0, keepdims=True)


def prepare_kernel(*refs, count):
    pick = refs[0]
    targets = refs[1 : 1 + count]
    left = refs[1 + count : 1 + 2 * count]
    wide = refs[1 + 2 * count :]
    own = targets[0].shape[1]
    both = jnp.concatenate([target[...] for target in targets], axis=1)
    feature = lax.dot_general(both, pick[...], TN, preferred_element_type=jnp.float32)
    for t in range(count):
        lines = slice(t * own, (t + 1) * own)
        left[t][...] = feature[lines, : 2 * FEAT].astype(jnp.bfloat16)
        wide[t][...] = feature[lines, 2 * FEAT :]


def sum_kernel(*refs, slots, blocks, numbers):
    ns, count = len(numbers), len(slots)
    refs = list(refs)

    def take(amount):
        taken = refs[:amount]
        del refs[:amount]
        return taken

    mask = take(1)[0]
    left, wide = take(count), take(count)
    sources = take(ns)
    begin, out = take(count), take(count)
    facing, back, fwd_tile, adj_tile = take(2), take(2), take(2), take(2)
    stack, geo, slabs, scale_q = refs
    own = out[0].shape[1]
    cases = out[0].shape[0] // 2
    per = own // BLK
    def match(slot, source):
        slab = slabs[slot, :, :].astype(jnp.bfloat16)
        right = jnp.concatenate([slab, slab, slab, jnp.ones_like(slab)], axis=0)

        def piece(t, which):
            cols = slice(FEAT, 2 * FEAT) if which else slice(0, FEAT)
            (back if which else facing)[slot][t * own : (t + 1) * own, :] = jnp.dot(
                left[t][:, cols], right, preferred_element_type=jnp.float32
            )

        return [functools.partial(piece, t, which) for t in range(count) for which in (0, 1)]

    def measure(slot, source):
        exact = source[2 * cases :, :].astype(jnp.float32)
        geo[slot, 0:3, :] = exact[0:3] + exact[3:6] + exact[6:9]
        area_q = exact[21:22] + exact[22:23] + exact[23:24]
        geo[slot, 3:4, :] = area_q
        flow = (exact[9:12] + exact[12:15] + exact[15:18]) * geo[slot, 0:3, :]
        offset = -(flow[0:1] + flow[1:2] + flow[2:3])
        slabs[slot, 0:GEO, :] = exact[0:GEO]
        slabs[slot, GEO:, :] = jnp.zeros((SLAB - GEO, own), jnp.float32)
        slabs[slot, WORD : WORD + 1, :] = offset - exact[18:19] - exact[19:20]
        scaled = area_q * (1.0 / math.pi)
        for number in range(-(-blocks // 8)):
            row = WORD if blocks <= 8 else GEO + number
            bits = min(8, blocks - 8 * number)
            power = jnp.exp2(-lax.broadcasted_iota(jnp.int32, (bits, own), 0).astype(jnp.float32))
            half = jnp.floor((exact[row : row + 1] + 0.5) * power)
            scale_q[slot, 8 * number : 8 * number + bits, :] = (half - 2.0 * jnp.floor(half * 0.5)) * scaled

    def build(k, slot, woven=()):
        spots, spot = count * own // ROWS, 0
        amount, done = len(woven), 0
        marks = []
        for jb in range(per):
            lanes = slice(jb * BLK, (jb + 1) * BLK)
            marks.append((lanes, [geo[slot, c : c + 1, lanes] for c in range(4)]))
        for t in range(count):
            for ib in range(per):
                row = slots[t] * per + ib
                pairs = [
                    (lanes, place, one_row(scale_q.at[slot], row, lanes), one_row(mask, k * blocks + row, lanes))
                    for lanes, place in marks
                ]
                for start in range(ib * BLK, (ib + 1) * BLK, ROWS):
                    here = slice(start, start + ROWS)
                    there = slice(t * own + start, t * own + start + ROWS)
                    x, y, z, area = (wide[t][here, c * BLK : (c + 1) * BLK] for c in range(4))
                    for lanes, (xq, yq, zq, aq), scale, sees in pairs:
                        dx = x - xq
                        dy = y - yq
                        dz = z - zq
                        square = dx * dx + dy * dy + dz * dz
                        faced = jnp.maximum(facing[slot][there, lanes], 0.0)
                        product = faced * jnp.maximum(back[slot][there, lanes], 0.0)
                        near = square + aq
                        far = square + area
                        fwd_tile[slot][there, lanes] = (product * scale / (near * near)).astype(jnp.bfloat16)
                        adj_tile[slot][there, lanes] = (product * sees * area / (far * far)).astype(jnp.bfloat16)
                    spot += 1
                    due = spot * amount // spots
                    while done < due:
                        woven[done]()
                        done += 1

    def collect(slot, source, onto):
        def piece(t, which):
            lines = slice(cases, 2 * cases) if which else slice(0, cases)
            tile = (adj_tile if which else fwd_tile)[slot][t * own : (t + 1) * own, :]
            out[t][lines, :] = onto[t][lines, :] + lax.dot_general(
                source[lines, :], tile, NT, preferred_element_type=jnp.float32
            )

        return [functools.partial(piece, t, which) for t in range(count) for which in (0, 1)]

    if ns <= 4:
        late = []
        for number, k in enumerate(numbers):
            if number == 0:
                measure(0, sources[0])
                for piece in match(0, sources[0]):
                    piece()
            if number + 1 < ns:
                measure((number + 1) % 2, sources[number + 1])
                late = late + match((number + 1) % 2, sources[number + 1])
            build(k, number % 2, late)
            late = collect(number % 2, sources[number], out if number else begin)
        for piece in late:
            piece()
    else:
        for i in range(ns):
            stack[i] = sources[i][...]
        for t in range(count):
            out[t][...] = begin[t][...]

        def step(i, _):
            source = stack.at[i]
            measure(0, source)
            for piece in match(0, source):
                piece()
            build(numbers[0] - i, 0)
            for piece in collect(0, source, out):
                piece()
            return 0

        lax.fori_loop(0, ns, step, 0)

def join_kernel(*refs):
    total = refs[0][...]
    for piece in refs[1:-1]:
        total = total + piece[...]
    refs[-1][...] = total


def finish_kernel(*refs, nr):
    emissivity, emission = refs[0:2]
    pieces = refs[2 : 2 + nr]
    radiosity_out, adjoint_out, gradient = refs[2 + nr :]
    cases = emission.shape[0]
    total = pieces[0][...]
    for piece in pieces[1:]:
        total = total + piece[...]
    incoming = total[0:cases]
    returned = total[cases:]
    mine = emissivity[...]
    power = emission[...]
    radiosity_out[...] = mine * power + (1.0 - mine) * incoming
    adjoint_out[...] = returned
    gradient[...] = jnp.sum(returned * (power - incoming), axis=0, keepdims=True)


def busy(micros):
    return pl.CostEstimate(flops=int(micros * 1.1e9), bytes_accessed=0, transcendentals=0)


def swap(x, axis, other):
    if other == 0:
        return x
    return lax.ppermute(x, axis, [(i, i ^ other) for i in range(lax.axis_size(axis))])


def local(
    positions,
    angles,
    areas,
    emissivity,
    emission,
    radiosity_in,
    adjoint_in,
    visibility,
    inlet_patches,
    inlet_weights,
):
    nz = lax.axis_size("emit")
    nr = lax.axis_size("recv")
    own = areas.shape[0]
    cases = emission.shape[0]
    per = own // BLK
    ids = inlet_patches.reshape(1, -1)
    vmem = pl.BlockSpec(memory_space=pltpu.VMEM)
    hbm = pl.BlockSpec(memory_space=pltpu.HBM)
    small = pltpu.CompilerParams(vmem_limit_bytes=4 << 20)
    f32 = jnp.float32
    blocks = nr * per
    extra = 0 if blocks <= 8 else -(-blocks // 64) * 8
    rows = 2 * cases + GEO + extra
    given = (
        positions,
        angles,
        areas.reshape(1, own),
        emissivity.reshape(1, own),
        radiosity_in,
        adjoint_in,
        emission,
        ids,
        inlet_weights,
        jnp.asarray(selection(), jnp.bfloat16),
    )
    given = tuple(pltpu.with_memory_space_constraint(x, pltpu.HBM) for x in given)
    seen = pltpu.with_memory_space_constraint(visibility, pltpu.HBM)
    packed = pl.pallas_call(
        functools.partial(pack_kernel, nr=nr, nz=nz, held=len(given)),
        out_shape=(jax.ShapeDtypeStruct((SLAB, own), jnp.bfloat16),)
        + (jax.ShapeDtypeStruct((rows, own), jnp.bfloat16),) * nz
        + tuple(jax.ShapeDtypeStruct(given[i].shape, given[i].dtype) for i in (3, 6, 7, 8, 9))
        + (jax.ShapeDtypeStruct((nz * blocks, own), f32),),
        in_specs=[hbm] * (1 + len(given)),
        out_specs=(vmem,) * (1 + nz + 6),
        scratch_shapes=[
            pltpu.VMEM((3, own), f32),
            pltpu.VMEM((2, own), f32),
            pltpu.VMEM((1, own), f32),
            pltpu.VMEM((cases, own), f32),
            pltpu.VMEM((cases, own), f32),
            pltpu.VMEM((nz, GEO + extra, own), f32),
            pltpu.SMEM(visibility.shape, jnp.int32),
            pltpu.SemaphoreType.DMA((len(given),)),
            pltpu.SemaphoreType.DMA,
        ],
        compiler_params=small,
    )(seen, *given)
    mine, power, ids, weights, pick, mask = packed[1 + nz :]
    targets = []
    for s in range(nr):
        targets.append(swap(targets[s - 1], "recv", 1) if s % 2 else swap(packed[0], "recv", s))
    sources = {k: swap(packed[1 + k], "emit", k) for k in reversed(range(nz))}
    source = pl.pallas_call(
        source_kernel,
        out_shape=jax.ShapeDtypeStruct((2 * cases, own), f32),
        in_specs=[vmem] * 2,
        out_specs=vmem,
        compiler_params=small,
        cost_estimate=busy(0.5),
    )(ids, weights)
    sums = jax.ShapeDtypeStruct((2 * cases, own), f32)
    zero = jnp.zeros((2 * cases, own), f32)

    left_kind = jax.ShapeDtypeStruct((own, 2 * FEAT), jnp.bfloat16)
    wide_kind = jax.ShapeDtypeStruct((own, 4 * BLK), f32)

    def prepare(chosen):
        count = len(chosen)
        made = pl.pallas_call(
            functools.partial(prepare_kernel, count=count),
            out_shape=(left_kind,) * count + (wide_kind,) * count,
            in_specs=[vmem] * (1 + count),
            out_specs=(vmem,) * (2 * count),
            compiler_params=pltpu.CompilerParams(vmem_limit_bytes=(2 + 3 * count) << 20),
            cost_estimate=busy(0.2 * count),
        )(pick, *chosen)
        return list(zip(made[:count], made[count:]))

    def add(slots, numbers, begin):
        count, ns = len(slots), len(numbers)
        return list(
            pl.pallas_call(
                functools.partial(sum_kernel, slots=slots, blocks=blocks, numbers=numbers),
                out_shape=(sums,) * count,
                in_specs=[vmem] * (1 + 3 * count + ns),
                out_specs=(vmem,) * count,
                scratch_shapes=[
                    *[pltpu.VMEM((count * own, own), f32)] * 4,
                    *[pltpu.VMEM((count * own, own), jnp.bfloat16)] * 4,
                    pltpu.VMEM((ns if ns > 4 else 1, rows, own), jnp.bfloat16),
                    pltpu.VMEM((2, 8, own), f32),
                    pltpu.VMEM((2, SLAB, own), f32),
                    pltpu.VMEM((2, blocks, own), f32),
                ],
                compiler_params=pltpu.CompilerParams(vmem_limit_bytes=12 << 20),
                cost_estimate=busy(0.3 * count * ns),
            )(
                mask,
                *[shapes[t][0] for t in slots],
                *[shapes[t][1] for t in slots],
                *[sources[k] for k in numbers],
                *begin,
            )
        )

    shapes = prepare(targets[:2]) + prepare(targets[2:])
    rest = tuple(range(nz - 1, 0, -1))
    begun = []
    for first in range(0, nr, 2):
        begun += add((first, first + 1), (0,), [zero if first else source, zero])
    far_sums = []
    for first in range(2, nr, 2):
        far_sums += add((first, first + 1), rest, begun[first : first + 2])
    far_sums, near_sums = lax.optimization_barrier((far_sums, begun[:2]))
    near_sums = add((0, 1), rest, near_sums)
    far = pl.pallas_call(
        join_kernel,
        out_shape=sums,
        in_specs=[vmem] * (nr - 2),
        out_specs=vmem,
        compiler_params=small,
        cost_estimate=busy(8.0),
    )(*[swap(far_sums[s - 2], "recv", s) for s in reversed(range(2, nr))])
    pieces = [far, near_sums[0], swap(near_sums[1], "recv", 1)]
    whole = jax.ShapeDtypeStruct((cases, own), f32)
    radiosity_out, adjoint_out, gradient = pl.pallas_call(
        functools.partial(finish_kernel, nr=len(pieces)),
        out_shape=(whole, whole, jax.ShapeDtypeStruct((1, own), f32)),
        in_specs=[vmem] * (2 + len(pieces)),
        out_specs=(vmem, vmem, vmem),
        compiler_params=small,
    )(mine, power, *pieces)
    return radiosity_out, adjoint_out, gradient.reshape(own)


def solution(mesh):
    patch = ("groups", "emit", "recv")
    placed = (
        P(None, patch),
        P(None, patch),
        P(patch),
        P(patch),
        P(None, patch),
        P(None, patch),
        P(None, patch),
        P(("groups", "emit"), None),
        P("groups"),
        P(None, "groups"),
    )
    return jax.shard_map(
        local,
        mesh=mesh,
        in_specs=placed,
        out_specs=(P(None, patch), P(None, patch), P(patch)),
        check_vma=False,
    )
```
